512 devices in a mesh: domain: 64 (over x, y, z_lo), member: 8 (over z_hi, core).
Axes of the slice: x: 4, y: 4, z: 16 (z_hi: 4, z_lo: 4; z = z_hi * 4 + z_lo), core: 2. Of those that a mesh axis runs over, the one named last changes fastest.
Arguments:
- inputs: bfloat16 [16, 12288, 1024], P('member', 'domain')
- norm_gain: bfloat16 [1024], P('member'), may hold values from 0.099609375 to 1.8984375
- w_query: bfloat16 [1024, 512], P('member')
- w_key: bfloat16 [1024, 512], P('member')
- w_value: bfloat16 [1024, 512], P('member'), may hold values from -0.1875 to 0.1875
- w_out: bfloat16 [512, 1024], P('member'), may hold values from -0.75 to 0.75
- neighbors: int32 [192, 9], P('domain'), may hold values from 0 to 191, as said below
- slot_valid: int32 [192, 9], P('domain'), may hold values from 0 to 1, as said below
- output_cotangent: bfloat16 [16, 12288, 1024], P('member', 'domain'), may hold values from -1.5 to 1.5
Outputs:
- attn_out: bfloat16 [16, 12288, 1024], P('member', 'domain')
- d_input: bfloat16 [16, 12288, 1024], P('member', 'domain')
- grad_wout: float32 [512, 1024], P('member')
The draws below stay inside these ranges and needn't reach their ends.
Inputs may be any that keep to these rules, and one draw needn't show every extreme that they name: `neighbors`: slot 0 of block b names b. The blocks named by the valid slots of b are distinct and lie within blocks (b // 3 - 1) * 3 to (b // 3 + 2) * 3 - 1. An invalid slot names b. `slot_valid`: slot 0 is always 1.
All inputs are finite; a program needn't handle non-finite values.
Results may differ from the reference program's by a relative error of at most 0.019.
Values may be sent and summed in bfloat16 or wider, within the bound.
No kernel may reach another device: no remote copies, remote signals or barrier semaphores. Data moves between devices by JAX's collectives and lax.ppermute only.
A program may use at most 128 MiB of HBM per device.

```python
import jax
import jax.numpy as jnp
from jax import lax

D = 1024
HEADS = 8
HEAD_DIM = 64
BLOCK = 64
KN = 9
BLK_DEV = 3
NBLK = 192
TOKENS = 12288
MEMBERS = 16


def neighbor_tables(key):
    base = jax.random.fold_in(key, 7)
    window_span = 3 * BLK_DEV
    blocks = jnp.arange(NBLK, dtype=jnp.int32)
    group_index = blocks // BLK_DEV
    offsets = jnp.arange(window_span, dtype=jnp.int32)
    noise_bits = jax.random.randint(jax.random.fold_in(base, 1), (NBLK, window_span), 0, 1 << 20)
    priority = noise_bits * window_span + offsets[None, :]
    own_pos = BLK_DEV + blocks % BLK_DEV
    priority = jnp.where(offsets[None, :] == own_pos[:, None], -3, priority)
    priority = jnp.where(offsets[None, :] == 0, -2, priority)
    priority = jnp.where(offsets[None, :] == window_span - 1, -1, priority)
    ranking = jnp.argsort(priority, axis=1, stable=True)[:, :KN].astype(jnp.int32)
    candidate = (group_index[:, None] - 1) * BLK_DEV + ranking
    inside = jnp.logical_and(candidate >= 0, candidate < NBLK)
    corner = jax.random.randint(jax.random.fold_in(base, 2), (NBLK,), 0, 4) == 0
    dropped_slot = jax.random.randint(jax.random.fold_in(base, 3), (NBLK,), 3, KN)
    slot_ids = jnp.arange(KN, dtype=jnp.int32)
    dropped = jnp.logical_and(corner[:, None], slot_ids[None, :] == dropped_slot[:, None])
    valid_slot = jnp.logical_and(inside, jnp.logical_not(dropped))
    chosen_blocks = jnp.where(valid_slot, candidate, blocks[:, None])
    return (chosen_blocks.astype(jnp.int32), valid_slot.astype(jnp.int32))


def draw_neighbors(key, part):
    return neighbor_tables(key)[0]


def draw_slot_valid(key, part):
    return neighbor_tables(key)[1]


def query_key_pair(key):
    spread = (2.0 / D) ** 0.5
    hidden_width = HEADS * HEAD_DIM
    key_part = jax.random.normal(jax.random.fold_in(key, 31), (D, hidden_width), jnp.float32) * spread
    query_part = jax.random.normal(jax.random.fold_in(key, 32), (D, hidden_width), jnp.float32) * spread
    return (query_part, key_part)


def draw_w_query(key, part):
    return query_key_pair(key)[0].astype(jnp.bfloat16)


def draw_w_key(key, part):
    return query_key_pair(key)[1].astype(jnp.bfloat16)


def draw_inputs(key, part):
    full_shape = (MEMBERS, TOKENS, D)
    values = jax.random.normal(jax.random.fold_in(key, 21), full_shape, jnp.float32)
    return values.astype(jnp.bfloat16)


def block_scale(key, extent, pieces, smallest, high):
    factor_of = 1.0
    for position, parts in pieces:
        draws = jax.random.uniform(jax.random.fold_in(jax.random.fold_in(key, 6), position), (parts,), jnp.float32, smallest / len(pieces), high / len(pieces))
        factor_of = factor_of * jnp.repeat(jnp.exp(draws), extent[position] // parts).reshape((-1,) + (1,) * (len(extent) - 1 - position))
    return factor_of


def bell_draw(rng, shape, scale, most, pieces=(), kind=jnp.bfloat16):
    level = block_scale(rng, shape, pieces, -0.22, 0.18) if pieces else 1.0
    result = jax.random.normal(rng, shape, jnp.float32) * scale * level
    return jnp.minimum(jnp.maximum(result, -most), most).astype(kind)


def setup_inputs(seed: int = 0) -> dict:
    seeds = jax.random.split(jax.random.key(seed), 10)
    return {
        "inputs": draw_inputs(jax.random.fold_in(seeds[9], 71), 0),
        "norm_gain": jnp.clip(1.0 + 0.18 * jax.random.normal(seeds[1], (D,), jnp.float32), 0.099609375, 1.8984375).astype(jnp.bfloat16),
        "w_query": draw_w_query(jax.random.fold_in(seeds[9], 71), 0),
        "w_key": draw_w_key(jax.random.fold_in(seeds[9], 71), 0),
        "w_value": bell_draw(seeds[4], (D, HEADS * HEAD_DIM), D ** -0.5, 0.1875, ((0, 8),)),
        "w_out": bell_draw(seeds[5], (HEADS * HEAD_DIM, D), (HEADS * HEAD_DIM // 8) ** -0.5, 0.75, ((0, 8),)),
        "neighbors": draw_neighbors(jax.random.fold_in(seeds[9], 71), 0),
        "slot_valid": draw_slot_valid(jax.random.fold_in(seeds[9], 71), 0),
        "output_cotangent": bell_draw(seeds[8], (MEMBERS, TOKENS, D), 0.25, 1.5, ((0, 8), (1, 64))),
    }


EPSILON = 1e-06
MASKED = -1e+30

def reference(inputs, norm_gain, w_query, w_key, w_value, w_out, neighbors, slot_valid, output_cotangent):
    hidden_width = HEADS * HEAD_DIM
    score_scale = HEAD_DIM ** (-0.5)
    gain_float = norm_gain.astype(jnp.float32)
    key_mask = jnp.repeat(slot_valid > 0, BLOCK, axis=1)
    flat_index = neighbors.reshape(-1).astype(jnp.int32)
    query_group = (jnp.arange(NBLK, dtype=jnp.int32) // BLK_DEV)[:, None]
    target_group = neighbors.astype(jnp.int32) // BLK_DEV
    relation = (query_group - target_group + 1).astype(jnp.int32)
    segment_ids = (neighbors.astype(jnp.int32) * 3 + relation).reshape(-1)

    def listed(field):
        blocks_view = field.reshape(NBLK, BLOCK, hidden_width)
        taken = jnp.take(blocks_view, flat_index, axis=0)
        return taken.reshape(NBLK, KN * BLOCK, HEADS, HEAD_DIM).astype(jnp.float32)

    def combine_parts(slots):
        summed = jax.ops.segment_sum(slots, segment_ids, num_segments=NBLK * 3)
        summed = summed.reshape(NBLK, 3, BLOCK, hidden_width)
        lower_part = lax.optimization_barrier(summed[:, 0].astype(jnp.bfloat16)).astype(jnp.float32)
        upper_part = lax.optimization_barrier(summed[:, 2].astype(jnp.bfloat16)).astype(jnp.float32)
        total = summed[:, 1] + lower_part + upper_part
        return total.astype(jnp.bfloat16).reshape(TOKENS, hidden_width)

    def one_member(grad_sum, member_pair):
        member_in, member_dy = member_pair
        inputs_float = member_in.astype(jnp.float32)
        inverse_rms = lax.rsqrt(lax.optimization_barrier(jnp.mean(inputs_float * inputs_float, axis=-1, keepdims=True)) + EPSILON)
        normalized_input = (inputs_float * inverse_rms * gain_float).astype(jnp.bfloat16)
        query = jnp.dot(normalized_input, w_query, preferred_element_type=jnp.float32).astype(jnp.bfloat16)
        key_rows = jnp.dot(normalized_input, w_key, preferred_element_type=jnp.float32).astype(jnp.bfloat16)
        value_rows = jnp.dot(normalized_input, w_value, preferred_element_type=jnp.float32).astype(jnp.bfloat16)
        query_blocks = query.reshape(NBLK, BLOCK, HEADS, HEAD_DIM).astype(jnp.float32)
        key_blocks = listed(key_rows)
        value_blocks = listed(value_rows)
        scores = jnp.einsum('bqhd,bkhd->bhqk', query_blocks, key_blocks) * score_scale
        scores = jnp.where(key_mask[:, None, None, :], scores, MASKED)
        row_max = lax.optimization_barrier(jnp.max(scores, axis=-1, keepdims=True))
        shifted = jnp.exp(scores - row_max)
        probability = shifted / lax.optimization_barrier(jnp.sum(shifted, axis=-1, keepdims=True))
        prob_bf = probability.astype(jnp.bfloat16)
        neighbour_attention = jnp.einsum('bhqk,bkhd->bqhd', prob_bf.astype(jnp.float32), value_blocks)
        neighbour_attention = neighbour_attention.astype(jnp.bfloat16).reshape(TOKENS, hidden_width)
        member_out = jnp.dot(neighbour_attention, w_out, preferred_element_type=jnp.float32).astype(jnp.bfloat16)
        d_attention = jnp.dot(member_dy, w_out.T, preferred_element_type=jnp.float32).astype(jnp.bfloat16)
        grad_sum = grad_sum + jnp.dot(neighbour_attention.T, member_dy, preferred_element_type=jnp.float32)
        d_att_blocks = d_attention.reshape(NBLK, BLOCK, HEADS, HEAD_DIM).astype(jnp.float32)
        d_prob = jnp.einsum('bqhd,bkhd->bhqk', d_att_blocks, value_blocks)
        delta = lax.optimization_barrier(jnp.sum(probability * d_prob, axis=-1, keepdims=True))
        d_score = (probability * (d_prob - delta) * score_scale).astype(jnp.bfloat16).astype(jnp.float32)
        query_cotangent = jnp.einsum('bhqk,bkhd->bqhd', d_score, key_blocks).astype(jnp.bfloat16).reshape(TOKENS, hidden_width)
        key_slots = jnp.einsum('bhqk,bqhd->bkhd', d_score, query_blocks).reshape(NBLK * KN, BLOCK, hidden_width)
        value_slots = jnp.einsum('bhqk,bqhd->bkhd', prob_bf.astype(jnp.float32), d_att_blocks).reshape(NBLK * KN, BLOCK, hidden_width)
        key_cotangent = combine_parts(key_slots)
        value_cotangent = combine_parts(value_slots)
        normed_cotangent = jnp.dot(query_cotangent, w_query.T, preferred_element_type=jnp.float32)
        normed_cotangent = normed_cotangent + jnp.dot(key_cotangent, w_key.T, preferred_element_type=jnp.float32)
        normed_cotangent = normed_cotangent + jnp.dot(value_cotangent, w_value.T, preferred_element_type=jnp.float32)
        scaled_grad = normed_cotangent * gain_float
        inner_mean = lax.optimization_barrier(jnp.mean(scaled_grad * inputs_float, axis=-1, keepdims=True))
        member_dx = inverse_rms * scaled_grad - inputs_float * inverse_rms ** 3 * inner_mean
        return (grad_sum, (member_out, member_dx.astype(jnp.bfloat16)))
    start_grad = jnp.zeros((hidden_width, D), jnp.float32)
    grad_sum, outputs = lax.scan(one_member, start_grad, (inputs, output_cotangent))
    attn_out, d_input = outputs
    return (attn_out, d_input, grad_sum / MEMBERS)
```

```python
import jax
import jax.numpy as jnp
from jax import lax
from jax.experimental import pallas as pl
from jax.experimental.pallas import tpu as pltpu
from jax.sharding import Mesh
from jax.sharding import PartitionSpec as P


HEAD_DIM = 64
PAIR = 2 * HEAD_DIM
EPSILON = 1e-06
MASKED = -1e30
X, Y, ZL, ZH, CORE = "x", "y", "zl", "zh", "core"
DOMAIN = (X, Y, ZL)
MEMBER = (ZH, CORE)
PLANE = (X, Y)
COLUMN = (ZL, ZH)
BF16, F32 = jnp.bfloat16, jnp.float32


def contract(a, b, da, db):
    return lax.dot_general(a, b, (((da,), (db,)), ((), ())), preferred_element_type=F32)


def attention_kernel(
    bias_ref, q_ref, k_ref, v_ref, g_ref, att_ref, dq_ref, low_ref, own_ref, high_ref
):
    rows = q_ref.shape[1]
    span = k_ref.shape[1]
    near = lax.broadcasted_iota(jnp.int32, (1, PAIR), 1) < HEAD_DIM

    def stacked(both):
        zero = jnp.zeros_like(both)
        return jnp.concatenate([jnp.where(near, both, zero), jnp.where(near, zero, both)], axis=0)

    def merged(columns):
        both = columns.T
        return jnp.where(near, both[:rows], both[rows:])

    query, key, value, grad = (stacked(q_ref[0]), k_ref[0], v_ref[0], stacked(g_ref[0]))
    blocks = bias_ref.shape[0]
    scores = contract(key, query, 1, 1).reshape(blocks, span // blocks, 2 * rows)
    scores = (scores + bias_ref[...]).reshape(span, 2 * rows)
    shifted = jnp.exp(scores - jnp.max(scores, axis=0, keepdims=True))
    prob = shifted * (1.0 / jnp.sum(shifted, axis=0, keepdims=True))
    prob_bf = prob.astype(BF16)
    att_ref[0] = merged(contract(value, prob_bf, 0, 0)).astype(BF16)
    d_prob = contract(value, grad, 1, 1)
    delta = jnp.sum(prob * d_prob, axis=0, keepdims=True)
    d_score = (prob * (d_prob - delta)).astype(BF16)
    dq_ref[0] = (merged(contract(key, d_score, 0, 0)) * HEAD_DIM**-0.5).astype(BF16)
    third = span // 3
    for part, total in enumerate((contract(d_score, query, 1, 0), contract(prob_bf, grad, 1, 0))):
        low_ref[part, 0] = total[:third].astype(BF16)
        own_ref[part, 0] = total[third : 2 * third]
        high_ref[part, 0] = total[2 * third :].astype(BF16)


def attention(bias, query, key_value, grad):
    samples, rows, width = query.shape
    span = key_value.shape[1]
    pairs = width // PAIR
    shape = jax.ShapeDtypeStruct
    narrow = pl.BlockSpec((1, rows, PAIR), lambda s, h: (s, 0, h))
    split = pl.BlockSpec((2, 1, rows, PAIR), lambda s, h: (0, s, 0, h))
    return pl.pallas_call(
        attention_kernel,
        grid=(samples, pairs),
        in_specs=[
            pl.BlockSpec(bias.shape, lambda s, h: (0, 0, 0)),
            narrow,
            pl.BlockSpec((1, span, PAIR), lambda s, h: (s, 0, h)),
            pl.BlockSpec((1, span, PAIR), lambda s, h: (s, 0, h + pairs)),
            narrow,
        ],
        out_specs=[narrow, narrow, split, split, split],
        out_shape=[
            shape((samples, rows, width), BF16),
            shape((samples, rows, width), BF16),
            shape((2, samples, rows, width), BF16),
            shape((2, samples, rows, width), F32),
            shape((2, samples, rows, width), BF16),
        ],
        cost_estimate=pl.CostEstimate(
            flops=12 * samples * rows * span * width,
            transcendentals=samples * rows * span * width // HEAD_DIM,
            bytes_accessed=16 * samples * rows * width,
        ),
        compiler_params=pltpu.CompilerParams(vmem_limit_bytes=48 * 2**20),
    )(bias, query, key_value, key_value, grad)


def column_gather(part):
    count = lax.axis_size(ZH)
    place = lax.axis_index(ZH)
    pieces = [part] + [
        lax.ppermute(part, ZH, [(i, (i + step) % count) for i in range(count)])
        for step in range(1, count)
    ]
    turned = jnp.stack(pieces[::-1] * 2)
    return lax.dynamic_slice_in_dim(turned, count - 1 - place, count, 0)


def other_core(value):
    return lax.ppermute(value, CORE, [(0, 1), (1, 0)])


def both_cores(mine):
    theirs = other_core(mine)
    first = lax.axis_index(CORE) == 0
    return jnp.stack([jnp.where(first, mine, theirs), jnp.where(first, theirs, mine)])


def plane_gather(piece):
    count = lax.axis_size(PLANE)
    copies = jnp.broadcast_to(piece[None], (count,) + piece.shape)
    return lax.all_to_all(copies, PLANE, 0, 0, tiled=True)


def gathered_weights(norm_gain, w_query, w_key, w_value, w_out):
    nx, ny, nz = (lax.axis_size(X), lax.axis_size(Y), lax.axis_size(ZH))
    xi, yi = (lax.axis_index(X), lax.axis_index(Y))
    depth, hidden_width = w_query.shape
    out_depth, model_width = w_out.shape
    rows = depth // (nx * ny)
    start = (xi * ny + yi) * rows
    out_rows, out_columns = (out_depth // nx, model_width // ny)
    out_part = lax.dynamic_slice(w_out, (xi * out_rows, yi * out_columns), (out_rows, out_columns))
    folds = out_rows // rows
    part = [lax.dynamic_slice_in_dim(w, start, rows, 0) for w in (w_query, w_key, w_value)]
    part += [out_part[i * rows : (i + 1) * rows] for i in range(folds)]
    part += [jnp.broadcast_to(norm_gain[None], (rows, depth))]
    part = column_gather(jnp.concatenate(part, axis=1))
    width = 3 * hidden_width + folds * out_columns
    gain = both_cores(part[:, :, width:])[:, :, 0]
    gain = jnp.swapaxes(gain, 0, 1).reshape(-1)
    whole = plane_gather(part[:, :, :width])
    whole = both_cores(whole)
    joint = jnp.transpose(whole[..., : 3 * hidden_width], (2, 0, 1, 3, 4))
    joint = joint.reshape(2 * nz * depth, 3 * hidden_width)
    whole = whole.reshape(2, nx, ny, nz, rows, width)
    bands = []
    for i in range(folds):
        begin = 3 * hidden_width + i * out_columns
        bands.append(jnp.transpose(whole[..., begin : begin + out_columns], (2, 3, 0, 1, 4, 5)))
    bands = jnp.stack(bands, axis=4).reshape(ny, 2 * nz * out_depth, out_columns)
    out_whole = jnp.concatenate([bands[i] for i in range(ny)], axis=1)
    return gain, joint, out_whole


def halved_gradient(attended, cotangent):
    nz = lax.axis_size(ZH)
    partial = jnp.einsum("sre,sru->eu", attended, cotangent, preferred_element_type=F32)
    width, model_width = partial.shape
    partial = partial.reshape(nz, 2, width // (2 * nz), model_width)
    first = lax.axis_index(CORE) == 0
    kept = jnp.where(first, partial[:, 0], partial[:, 1])
    sent = jnp.where(first, partial[:, 1], partial[:, 0])
    return (kept + other_core(sent)).astype(BF16)


def summed_gradient(half, total_samples):
    nx, ny, nz, nl = (lax.axis_size(X), lax.axis_size(Y), lax.axis_size(ZH), lax.axis_size(ZL))
    _, share, model_width = half.shape
    rows, columns = (share // nx, model_width // ny)
    half = jnp.stack([half[:, :, i * columns : (i + 1) * columns] for i in range(ny)])
    half = jnp.swapaxes(half.reshape(ny, nz, nx, rows, columns), 1, 2)
    half = half.reshape(ny * nx, nz, rows, columns)
    half = lax.all_to_all(half, (Y, X), 0, 0, tiled=True)
    part = jnp.sum(half.astype(F32), axis=0)
    part = jnp.broadcast_to(part[None], (nl, nz, rows, columns)).reshape(nl * nz, rows, columns)
    part = lax.all_to_all(part, COLUMN, 0, 0, tiled=True)
    part = jnp.sum(part, axis=0) / total_samples
    whole = plane_gather(part).reshape(nx, ny, rows, columns)
    return jnp.concatenate([whole[:, i].reshape(share, columns) for i in range(ny)], axis=1)


def shards(
    inputs, norm_gain, w_query, w_key, w_value, w_out, neighbors, slot_valid, output_cotangent
):
    samples, length, _ = inputs.shape
    block_count, _ = neighbors.shape
    block_len = length // block_count
    window_blocks = 3 * block_count
    groups = lax.axis_size(DOMAIN)
    up = [(i, i + 1) for i in range(groups - 1)]
    down = [(j, i) for i, j in up]
    below = lax.ppermute(inputs, DOMAIN, up)
    above = lax.ppermute(inputs, DOMAIN, down)
    gain, w_joint, w_full_out = gathered_weights(norm_gain, w_query, w_key, w_value, w_out)
    hidden_width = w_query.shape[1]
    gain_float = gain.astype(F32)

    def normalized(rows):
        rows = rows.astype(F32)
        inverse = lax.rsqrt(jnp.mean(rows * rows, axis=-1, keepdims=True) + EPSILON)
        return inverse, (rows * inverse * gain_float).astype(BF16)

    inverse_rms, normed = normalized(inputs)
    _, window = normalized(jnp.concatenate([below, inputs, above], axis=1))
    query = jnp.einsum(
        "sti,iy->sty", normed, w_joint[:, :hidden_width], preferred_element_type=F32
    ).astype(BF16) * jnp.asarray(HEAD_DIM**-0.5, BF16)
    key_value = jnp.einsum(
        "sti,iy->sty", window, w_joint[:, hidden_width:], preferred_element_type=F32
    ).astype(BF16)
    d_attention = jnp.einsum(
        "stz,yz->sty", output_cotangent, w_full_out, preferred_element_type=F32
    ).astype(BF16)

    group = lax.axis_index(DOMAIN)
    local_index = neighbors - (group - 1) * block_count
    matches = jnp.logical_and(
        local_index[:, :, None] == jnp.arange(window_blocks, dtype=jnp.int32)[None, None, :],
        (slot_valid > 0)[:, :, None],
    )
    bias = jnp.where(jnp.any(matches, axis=1).T, 0.0, MASKED).astype(F32)
    bias = jnp.tile(jnp.repeat(bias, block_len, axis=1), (1, 2))[:, None, :]

    attended, d_query, low, own, high = attention(bias, query, key_value, d_attention)
    half = halved_gradient(attended, output_cotangent)
    half, low, high, attended = lax.optimization_barrier((half, low, high, attended))
    from_below = lax.ppermute(high, DOMAIN, up)
    from_above = lax.ppermute(low, DOMAIN, down)
    attn_out = jnp.einsum(
        "sty,yb->stb", attended, w_full_out, preferred_element_type=F32
    ).astype(BF16)
    members = lax.axis_size(MEMBER)
    grad_wout = summed_gradient(half, samples * members)
    d_key_value = (own + from_below.astype(F32) + from_above.astype(F32)).astype(BF16)
    d_joint = jnp.concatenate([d_query, d_key_value[0], d_key_value[1]], axis=-1)
    d_normed = jnp.einsum("sty,iy->sti", d_joint, w_joint, preferred_element_type=F32)
    inputs_float = inputs.astype(F32)
    scaled = d_normed * gain_float
    inner = jnp.mean(scaled * inputs_float, axis=-1, keepdims=True)
    d_input = inverse_rms * scaled - inputs_float * inverse_rms**3 * inner
    return attn_out, d_input.astype(BF16), grad_wout


def solution(mesh):
    fine = Mesh(mesh.devices.reshape(4, 4, 4, 4, 2), (X, Y, ZL, ZH, CORE))
    placed = (
        P(MEMBER, DOMAIN, None),
        P(MEMBER),
        P(MEMBER, None),
        P(MEMBER, None),
        P(MEMBER, None),
        P(MEMBER, None),
        P(DOMAIN, None),
        P(DOMAIN, None),
        P(MEMBER, DOMAIN, None),
    )

    return jax.shard_map(
        shards,
        mesh=fine,
        in_specs=placed,
        out_specs=(P(MEMBER, DOMAIN, None), P(MEMBER, DOMAIN, None), P(MEMBER, None)),
        check_vma=False,
    )
```

```python
import jax
import jax.numpy as jnp
from jax import lax
from jax.experimental import pallas as pl
from jax.experimental.pallas import tpu as pltpu
from jax.sharding import Mesh
from jax.sharding import PartitionSpec as P


HEAD_DIM = 64
PAIR = 2 * HEAD_DIM
EPSILON = 1e-06
MASKED = -1e30
X, Y, ZL, ZH, CORE = "x", "y", "zl", "zh", "core"
DOMAIN = (X, Y, ZL)
MEMBER = (ZH, CORE)
PLANE = (X, Y)
COLUMN = (ZL, ZH)
BF16, F32 = jnp.bfloat16, jnp.float32


def contract(a, b, da, db):
    return lax.dot_general(a, b, (((da,), (db,)), ((), ())), preferred_element_type=F32)


def head_lanes():
    return lax.broadcasted_iota(jnp.int32, (1, PAIR), 1) < HEAD_DIM


def stacked(both):
    near = head_lanes()
    zero = jnp.zeros_like(both)
    return jnp.concatenate([jnp.where(near, both, zero), jnp.where(near, zero, both)], axis=0)


def merged(columns):
    both = columns.T
    rows = both.shape[0] // 2
    return jnp.where(head_lanes(), both[:rows], both[rows:])


def masked_scores(bias_ref, key, query):
    blocks = bias_ref.shape[0]
    span, columns = (key.shape[0], query.shape[0])
    scores = contract(key, query, 1, 1).reshape(blocks, span // blocks, columns)
    return (scores + bias_ref[...]).reshape(span, columns)


def forward_kernel(bias_ref, q_ref, k_ref, v_ref, att_ref, stat_ref):
    scores = masked_scores(bias_ref, k_ref[0], stacked(q_ref[0]))
    row_max = jnp.max(scores, axis=0, keepdims=True)
    shifted = jnp.exp(scores - row_max)
    inverse = 1.0 / jnp.sum(shifted, axis=0, keepdims=True)
    prob_bf = (shifted * inverse).astype(BF16)
    att_ref[0] = merged(contract(v_ref[0], prob_bf, 0, 0)).astype(BF16)
    stat_ref[0, 0, 0:1, :] = row_max
    stat_ref[0, 0, 1:2, :] = inverse


def backward_kernel(
    bias_ref, q_ref, k_ref, v_ref, g_ref, stat_ref, dq_ref, low_ref, own_ref, high_ref
):
    query, key, value, grad = (stacked(q_ref[0]), k_ref[0], v_ref[0], stacked(g_ref[0]))
    span = key.shape[0]
    scores = masked_scores(bias_ref, key, query)
    prob = jnp.exp(scores - stat_ref[0, 0, 0:1, :]) * stat_ref[0, 0, 1:2, :]
    prob_bf = prob.astype(BF16)
    d_prob = contract(value, grad, 1, 1)
    delta = jnp.sum(prob * d_prob, axis=0, keepdims=True)
    d_score = (prob * (d_prob - delta)).astype(BF16)
    dq_ref[0] = (merged(contract(key, d_score, 0, 0)) * HEAD_DIM**-0.5).astype(BF16)
    third = span // 3
    for part, total in enumerate((contract(d_score, query, 1, 0), contract(prob_bf, grad, 1, 0))):
        low_ref[part, 0] = total[:third].astype(BF16)
        own_ref[part, 0] = total[third : 2 * third]
        high_ref[part, 0] = total[2 * third :].astype(BF16)


def attention_specs(bias, query, key_value):
    samples, rows, width = query.shape
    span = key_value.shape[1]
    pairs = width // PAIR
    narrow = pl.BlockSpec((1, rows, PAIR), lambda s, h: (s, 0, h))
    given = [
        pl.BlockSpec(bias.shape, lambda s, h: (0, 0, 0)),
        narrow,
        pl.BlockSpec((1, span, PAIR), lambda s, h: (s, 0, h)),
        pl.BlockSpec((1, span, PAIR), lambda s, h: (s, 0, h + pairs)),
    ]
    stat = pl.BlockSpec((1, 1, 2, 2 * rows), lambda s, h: (s, h, 0, 0))
    stat_shape = jax.ShapeDtypeStruct((samples, pairs, 2, 2 * rows), F32)
    return (samples, pairs), given, narrow, stat, stat_shape


def attention_cost(query, key_value, products):
    samples, rows, width = query.shape
    span = key_value.shape[1]
    return pl.CostEstimate(
        flops=2 * products * samples * rows * span * width,
        transcendentals=samples * rows * span * width // HEAD_DIM,
        bytes_accessed=3 * products * samples * rows * width,
    )


def forward_attention(bias, query, key_value):
    grid, given, narrow, stat, stat_shape = attention_specs(bias, query, key_value)
    return pl.pallas_call(
        forward_kernel,
        grid=grid,
        in_specs=given,
        out_specs=[narrow, stat],
        out_shape=[jax.ShapeDtypeStruct(query.shape, BF16), stat_shape],
        cost_estimate=attention_cost(query, key_value, 2),
        compiler_params=pltpu.CompilerParams(vmem_limit_bytes=40 * 2**20),
    )(bias, query, key_value, key_value)


def backward_attention(bias, query, key_value, grad, stats):
    grid, given, narrow, stat, _ = attention_specs(bias, query, key_value)
    samples, rows, width = query.shape
    shape = jax.ShapeDtypeStruct
    split = pl.BlockSpec((2, 1, rows, PAIR), lambda s, h: (0, s, 0, h))
    return pl.pallas_call(
        backward_kernel,
        grid=grid,
        in_specs=given + [narrow, stat],
        out_specs=[narrow, split, split, split],
        out_shape=[
            shape((samples, rows, width), BF16),
            shape((2, samples, rows, width), BF16),
            shape((2, samples, rows, width), F32),
            shape((2, samples, rows, width), BF16),
        ],
        cost_estimate=attention_cost(query, key_value, 5),
        compiler_params=pltpu.CompilerParams(vmem_limit_bytes=40 * 2**20),
    )(bias, query, key_value, key_value, grad, stats)


def slice_kernel(place_ref, q_ref, k_ref, v_ref, out_ref, gain_ref, part_ref):
    rows, width = q_ref.shape
    columns = out_ref.shape[1]
    folds = out_ref.shape[0] // rows
    for i, ref in enumerate((q_ref, k_ref, v_ref)):
        part_ref[:, i * width : (i + 1) * width] = ref[...]
    for i in range(folds):
        begin = 3 * width + i * columns
        part_ref[:, begin : begin + columns] = out_ref[i * rows : (i + 1) * rows, :]
    begin = 3 * width + folds * columns
    part_ref[:, begin:] = jnp.broadcast_to(gain_ref[...], (rows, gain_ref.shape[1]))


def own_slices(norm_gain, w_query, w_key, w_value, w_out, rows, out_rows, out_columns):
    depth, width = w_query.shape
    xi, yi = (lax.axis_index(X), lax.axis_index(Y))
    place = jnp.stack([xi * lax.axis_size(Y) + yi, xi, yi])
    band = pl.BlockSpec((rows, width), lambda i, place: (place[0], 0))
    total = 3 * width + out_rows // rows * out_columns + depth
    return pl.pallas_call(
        slice_kernel,
        grid_spec=pltpu.PrefetchScalarGridSpec(
            num_scalar_prefetch=1,
            grid=(1,),
            in_specs=[
                band,
                band,
                band,
                pl.BlockSpec((out_rows, out_columns), lambda i, place: (place[1], place[2])),
                pl.BlockSpec((1, depth), lambda i, place: (0, 0)),
            ],
            out_specs=pl.BlockSpec((rows, total), lambda i, place: (0, 0)),
        ),
        out_shape=jax.ShapeDtypeStruct((rows, total), BF16),
    )(place, w_query, w_key, w_value, w_out, norm_gain[None])


def column_gather(part):
    count = lax.axis_size(ZH)
    place = lax.axis_index(ZH)
    up = [(i, (i + 1) % count) for i in range(count)]
    down = [(j, i) for i, j in up]
    first = lax.ppermute(part, ZH, up)
    third = lax.ppermute(part, ZH, down)
    second = lax.ppermute(first, ZH, up)
    turned = jnp.stack([third, second, first, part] * 2)
    return lax.dynamic_slice_in_dim(turned, count - 1 - place, count, 0)


def other_core(value):
    return lax.ppermute(value, CORE, [(0, 1), (1, 0)])


def both_cores(mine):
    theirs = other_core(mine)
    first = lax.axis_index(CORE) == 0
    return jnp.stack([jnp.where(first, mine, theirs), jnp.where(first, theirs, mine)])


def plane_gather(piece):
    count = lax.axis_size(PLANE)
    copies = jnp.broadcast_to(piece[None], (count,) + piece.shape)
    return lax.all_to_all(copies, PLANE, 0, 0, tiled=True)


def gathered_weights(norm_gain, w_query, w_key, w_value, w_out):
    nx, ny, nz = (lax.axis_size(X), lax.axis_size(Y), lax.axis_size(ZH))
    depth, hidden_width = w_query.shape
    out_depth, model_width = w_out.shape
    rows = depth // (nx * ny)
    out_rows, out_columns = (out_depth // nx, model_width // ny)
    folds = out_rows // rows
    part = own_slices(norm_gain, w_query, w_key, w_value, w_out, rows, out_rows, out_columns)
    part = column_gather(part)
    width = 3 * hidden_width + folds * out_columns
    gain = both_cores(part[:, :, width:])[:, :, 0]
    gain = jnp.swapaxes(gain, 0, 1).reshape(-1)
    whole = plane_gather(part[:, :, :width])
    whole = both_cores(whole)
    joint = jnp.transpose(whole[..., : 3 * hidden_width], (2, 0, 1, 3, 4))
    joint = joint.reshape(2 * nz * depth, 3 * hidden_width)
    whole = whole.reshape(2, nx, ny, nz, rows, width)
    bands = []
    for i in range(folds):
        begin = 3 * hidden_width + i * out_columns
        bands.append(jnp.transpose(whole[..., begin : begin + out_columns], (2, 3, 0, 1, 4, 5)))
    bands = jnp.stack(bands, axis=4).reshape(ny, 2 * nz * out_depth, out_columns)
    out_whole = jnp.concatenate([bands[i] for i in range(ny)], axis=1)
    return gain, joint, out_whole


def halved_gradient(attended, cotangent):
    nz = lax.axis_size(ZH)
    partial = jnp.einsum("sre,sru->eu", attended, cotangent, preferred_element_type=F32)
    width, model_width = partial.shape
    partial = partial.reshape(nz, 2, width // (2 * nz), model_width)
    first = lax.axis_index(CORE) == 0
    kept = jnp.where(first, partial[:, 0], partial[:, 1])
    sent = jnp.where(first, partial[:, 1], partial[:, 0])
    return (kept + other_core(sent)).astype(BF16)


def summed_gradient(half, total_samples):
    nx, ny, nz, nl = (lax.axis_size(X), lax.axis_size(Y), lax.axis_size(ZH), lax.axis_size(ZL))
    _, share, model_width = half.shape
    rows, columns = (share // nx, model_width // ny)
    half = jnp.stack([half[:, :, i * columns : (i + 1) * columns] for i in range(ny)])
    half = jnp.swapaxes(half.reshape(ny, nz, nx, rows, columns), 1, 2)
    half = half.reshape(ny * nx, nz, rows, columns)
    half = lax.all_to_all(half, (Y, X), 0, 0, tiled=True)
    part = jnp.sum(half.astype(F32), axis=0)
    part = jnp.broadcast_to(part[None], (nl, nz, rows, columns)).reshape(nl * nz, rows, columns)
    part = lax.all_to_all(part, COLUMN, 0, 0, tiled=True)
    part = jnp.sum(part, axis=0) / total_samples
    whole = plane_gather(part).reshape(nx, ny, rows, columns)
    return jnp.concatenate([whole[:, i].reshape(share, columns) for i in range(ny)], axis=1)


def shards(
    inputs, norm_gain, w_query, w_key, w_value, w_out, neighbors, slot_valid, output_cotangent
):
    samples, length, _ = inputs.shape
    block_count, _ = neighbors.shape
    block_len = length // block_count
    window_blocks = 3 * block_count
    groups = lax.axis_size(DOMAIN)
    up = [(i, i + 1) for i in range(groups - 1)]
    down = [(j, i) for i, j in up]
    below = lax.ppermute(inputs, DOMAIN, up)
    above = lax.ppermute(inputs, DOMAIN, down)
    gain, w_joint, w_full_out = gathered_weights(norm_gain, w_query, w_key, w_value, w_out)
    hidden_width = w_query.shape[1]
    gain_float = gain.astype(F32)

    def normalized(rows):
        rows = rows.astype(F32)
        inverse = lax.rsqrt(jnp.mean(rows * rows, axis=-1, keepdims=True) + EPSILON)
        return inverse, (rows * inverse * gain_float).astype(BF16)

    inverse_rms, normed = normalized(inputs)
    _, window = normalized(jnp.concatenate([below, inputs, above], axis=1))
    query = jnp.einsum(
        "sti,iy->sty", normed, w_joint[:, :hidden_width], preferred_element_type=F32
    ).astype(BF16) * jnp.asarray(HEAD_DIM**-0.5, BF16)
    key_value = jnp.einsum(
        "sti,iy->sty", window, w_joint[:, hidden_width:], preferred_element_type=F32
    ).astype(BF16)
    d_attention = jnp.einsum(
        "stz,yz->sty", output_cotangent, w_full_out, preferred_element_type=F32
    ).astype(BF16)

    group = lax.axis_index(DOMAIN)
    local_index = neighbors - (group - 1) * block_count
    matches = jnp.logical_and(
        local_index[:, :, None] == jnp.arange(window_blocks, dtype=jnp.int32)[None, None, :],
        (slot_valid > 0)[:, :, None],
    )
    bias = jnp.where(jnp.any(matches, axis=1).T, 0.0, MASKED).astype(F32)
    bias = jnp.tile(jnp.repeat(bias, block_len, axis=1), (1, 2))[:, None, :]

    attended, stats = forward_attention(bias, query, key_value)
    half = halved_gradient(attended, output_cotangent)
    half, d_attention = lax.optimization_barrier((half, d_attention))
    members = lax.axis_size(MEMBER)
    grad_wout = summed_gradient(half, samples * members)
    d_query, low, own, high = backward_attention(bias, query, key_value, d_attention, stats)
    from_below = lax.ppermute(high, DOMAIN, up)
    from_above = lax.ppermute(low, DOMAIN, down)
    attended, own = lax.optimization_barrier((attended, own))
    attn_out = jnp.einsum(
        "sty,yb->stb", attended, w_full_out, preferred_element_type=F32
    ).astype(BF16)
    d_key_value = (own + from_below.astype(F32) + from_above.astype(F32)).astype(BF16)
    d_joint = jnp.concatenate([d_query, d_key_value[0], d_key_value[1]], axis=-1)
    d_normed = jnp.einsum("sty,iy->sti", d_joint, w_joint, preferred_element_type=F32)
    inputs_float = inputs.astype(F32)
    scaled = d_normed * gain_float
    inner = jnp.mean(scaled * inputs_float, axis=-1, keepdims=True)
    d_input = inverse_rms * scaled - inputs_float * inverse_rms**3 * inner
    return attn_out, d_input.astype(BF16), grad_wout


def solution(mesh):
    fine = Mesh(mesh.devices.reshape(4, 4, 4, 4, 2), (X, Y, ZL, ZH, CORE))
    placed = (
        P(MEMBER, DOMAIN, None),
        P(MEMBER),
        P(MEMBER, None),
        P(MEMBER, None),
        P(MEMBER, None),
        P(MEMBER, None),
        P(DOMAIN, None),
        P(DOMAIN, None),
        P(MEMBER, DOMAIN, None),
    )

    return jax.shard_map(
        shards,
        mesh=fine,
        in_specs=placed,
        out_specs=(P(MEMBER, DOMAIN, None), P(MEMBER, DOMAIN, None), P(MEMBER, None)),
        check_vma=False,
    )
```

```python
import jax
import jax.numpy as jnp
from jax import lax
from jax.experimental import pallas as pl
from jax.experimental.pallas import tpu as pltpu
from jax.sharding import Mesh
from jax.sharding import PartitionSpec as P


HEAD_DIM = 64
PAIR = 2 * HEAD_DIM
SCALE = HEAD_DIM**-0.5
EPSILON = 1e-06
MASKED = -1e30
X, Y, ZL, ZH, CORE = "x", "y", "zl", "zh", "core"
DOMAIN = (X, Y, ZL)
MEMBER = (ZH, CORE)
PLANE = (X, Y)
COLUMN = (ZL, ZH)
BF16, F32 = jnp.bfloat16, jnp.float32


def contract(a, b, da, db):
    return lax.dot_general(a, b, (((da,), (db,)), ((), ())), preferred_element_type=F32)


def head_lanes():
    return lax.broadcasted_iota(jnp.int32, (1, PAIR), 1) < HEAD_DIM


def stacked(both, scale=1.0):
    near = head_lanes()
    both = both * jnp.asarray(scale, both.dtype)
    zero = jnp.zeros_like(both)
    return jnp.concatenate([jnp.where(near, both, zero), jnp.where(near, zero, both)], axis=0)


def merged(columns):
    both = columns.T
    rows = both.shape[0] // 2
    return jnp.where(head_lanes(), both[:rows], both[rows:])


def masked_scores(bias, key, query):
    blocks = bias.shape[0]
    span, columns = (key.shape[0], query.shape[0])
    scores = contract(key, query, 1, 1).reshape(blocks, span // blocks, columns)
    return (scores + bias).reshape(span, columns)


def forward_kernel(bias_ref, q_ref, k_ref, v_ref, att_ref, stat_ref):
    scores = masked_scores(bias_ref[...], k_ref[0], stacked(q_ref[0], SCALE))
    row_max = jnp.max(scores, axis=0, keepdims=True)
    shifted = jnp.exp(scores - row_max)
    inverse = 1.0 / jnp.sum(shifted, axis=0, keepdims=True)
    prob_bf = (shifted * inverse).astype(BF16)
    att_ref[0] = merged(contract(v_ref[0], prob_bf, 0, 0)).astype(BF16)
    stat_ref[0, 0, 0:1, :] = row_max
    stat_ref[0, 0, 1:2, :] = inverse


def query_kernel(bias_ref, q_ref, k_ref, v_ref, g_ref, stat_ref, dq_ref, own_ref, all_ref):
    rows = q_ref.shape[1]
    query, key, value, grad = (stacked(q_ref[0], SCALE), k_ref[0], v_ref[0], stacked(g_ref[0]))
    row_max, inverse = (stat_ref[0, 0, 0:1, :], stat_ref[0, 0, 1:2, :])
    prob = jnp.exp(masked_scores(bias_ref[...], key, query) - row_max) * inverse
    d_prob = contract(value, grad, 1, 1)
    delta = jnp.sum(prob * d_prob, axis=0, keepdims=True)
    d_score = (prob * (d_prob - delta)).astype(BF16)
    dq_ref[0] = (merged(contract(key, d_score, 0, 0)) * SCALE).astype(BF16)
    own_ref[0, 0] = contract(d_score[rows : 2 * rows], query, 1, 0)
    own_ref[1, 0] = contract(prob[rows : 2 * rows].astype(BF16), grad, 1, 0)
    all_ref[0, 0, 0:1, :] = row_max
    all_ref[0, 0, 1:2, :] = inverse
    all_ref[0, 0, 2:3, :] = delta


def key_kernel(
    low_bias_ref,
    high_bias_ref,
    low_q_ref,
    high_q_ref,
    k_ref,
    v_ref,
    low_g_ref,
    high_g_ref,
    low_stat_ref,
    high_stat_ref,
    own_ref,
    dk_ref,
    dv_ref,
):
    key, value = (k_ref[0], v_ref[0])
    d_key, d_value = (own_ref[0, 0], own_ref[1, 0])
    sides = (
        (low_bias_ref, low_q_ref, low_g_ref, low_stat_ref),
        (high_bias_ref, high_q_ref, high_g_ref, high_stat_ref),
    )
    for bias_ref, q_ref, g_ref, stat_ref in sides:
        query, grad = (stacked(q_ref[0], SCALE), stacked(g_ref[0]))
        scores = masked_scores(bias_ref[...], key, query)
        prob = jnp.exp(scores - stat_ref[0, 0, 0:1, :]) * stat_ref[0, 0, 1:2, :]
        d_prob = contract(value, grad, 1, 1)
        d_score = (prob * (d_prob - stat_ref[0, 0, 2:3, :])).astype(BF16)
        d_key += contract(d_score, query, 1, 0)
        d_value += contract(prob.astype(BF16), grad, 1, 0)
    dk_ref[0] = d_key.astype(BF16)
    dv_ref[0] = d_value.astype(BF16)


class Plan:
    def __init__(self, joint):
        samples, span, width = joint.shape
        self.rows, self.width, self.span = (span // 3, width // 3, span)
        self.samples, self.pairs = (samples, width // 3 // PAIR)
        self.grid = (samples, self.pairs)
        self.narrow = pl.BlockSpec((1, self.rows, PAIR), lambda s, h: (s, 0, h))
        self.split = pl.BlockSpec((2, 1, self.rows, PAIR), lambda s, h: (0, s, 0, h))

    def joint(self, kind, third=None):
        first = kind * self.pairs
        if third is None:
            return pl.BlockSpec((1, self.span, PAIR), lambda s, h: (s, 0, h + first))
        return pl.BlockSpec((1, self.rows, PAIR), lambda s, h: (s, third, h + first))

    def bias(self, bias):
        return pl.BlockSpec(bias.shape, lambda s, h: (0, 0, 0))

    def stat(self, count):
        return pl.BlockSpec((1, 1, count, 2 * self.rows), lambda s, h: (s, h, 0, 0))

    def stat_shape(self, count):
        return jax.ShapeDtypeStruct((self.samples, self.pairs, count, 2 * self.rows), F32)

    def narrow_shape(self):
        return jax.ShapeDtypeStruct((self.samples, self.rows, self.width), BF16)

    def call(self, kernel, products, in_specs, out_specs, out_shape):
        work = self.samples * self.rows * self.span * self.width
        return pl.pallas_call(
            kernel,
            grid=self.grid,
            in_specs=in_specs,
            out_specs=out_specs,
            out_shape=out_shape,
            cost_estimate=pl.CostEstimate(
                flops=2 * products * work,
                transcendentals=work // HEAD_DIM,
                bytes_accessed=3 * products * self.samples * self.rows * self.width,
            ),
            compiler_params=pltpu.CompilerParams(vmem_limit_bytes=16 * 2**20),
        )


def forward_attention(bias, joint):
    plan = Plan(joint)
    given = [plan.bias(bias), plan.joint(0, 1), plan.joint(1), plan.joint(2)]
    outs = ([plan.narrow, plan.stat(2)], [plan.narrow_shape(), plan.stat_shape(2)])
    return plan.call(forward_kernel, 2, given, *outs)(bias, joint, joint, joint)


def query_gradient(bias, joint, grad, stats):
    plan = Plan(joint)
    given = [plan.bias(bias), plan.joint(0, 1), plan.joint(1), plan.joint(2)]
    given += [plan.narrow, plan.stat(2)]
    own = jax.ShapeDtypeStruct((2, plan.samples, plan.rows, plan.width), F32)
    outs = (
        [plan.narrow, plan.split, plan.stat(3)],
        [plan.narrow_shape(), own, plan.stat_shape(3)],
    )
    return plan.call(query_kernel, 4, given, *outs)(bias, joint, joint, joint, grad, stats)


def key_gradient(biases, joint, grads, stats, own):
    plan = Plan(joint)
    given = [plan.bias(biases[0]), plan.bias(biases[1]), plan.joint(0, 0), plan.joint(0, 2)]
    given += [plan.joint(1, 1), plan.joint(2, 1), plan.narrow, plan.narrow]
    given += [plan.stat(3), plan.stat(3), plan.split]
    outs = ([plan.narrow] * 2, [plan.narrow_shape()] * 2)
    call = plan.call(key_kernel, 3, given, *outs)
    return call(*biases, joint, joint, joint, joint, *grads, *stats, own)


def slice_kernel(place_ref, q_ref, k_ref, v_ref, out_ref, gain_ref, part_ref):
    rows, width = q_ref.shape
    columns = out_ref.shape[1]
    folds = out_ref.shape[0] // rows
    for i, ref in enumerate((q_ref, k_ref, v_ref)):
        part_ref[:, i * width : (i + 1) * width] = ref[...]
    for i in range(folds):
        begin = 3 * width + i * columns
        part_ref[:, begin : begin + columns] = out_ref[i * rows : (i + 1) * rows, :]
    begin = 3 * width + folds * columns
    part_ref[:, begin:] = jnp.broadcast_to(gain_ref[...], (rows, gain_ref.shape[1]))


def own_slices(norm_gain, w_query, w_key, w_value, w_out, rows, out_rows, out_columns):
    depth, width = w_query.shape
    xi, yi = (lax.axis_index(X), lax.axis_index(Y))
    place = jnp.stack([xi * lax.axis_size(Y) + yi, xi, yi])
    band = pl.BlockSpec((rows, width), lambda i, place: (place[0], 0))
    total = 3 * width + out_rows // rows * out_columns + depth
    return pl.pallas_call(
        slice_kernel,
        grid_spec=pltpu.PrefetchScalarGridSpec(
            num_scalar_prefetch=1,
            grid=(1,),
            in_specs=[
                band,
                band,
                band,
                pl.BlockSpec((out_rows, out_columns), lambda i, place: (place[1], place[2])),
                pl.BlockSpec((1, depth), lambda i, place: (0, 0)),
            ],
            out_specs=pl.BlockSpec((rows, total), lambda i, place: (0, 0)),
        ),
        out_shape=jax.ShapeDtypeStruct((rows, total), BF16),
    )(place, w_query, w_key, w_value, w_out, norm_gain[None])


def column_gather(part):
    count = lax.axis_size(ZH)
    place = lax.axis_index(ZH)
    up = [(i, (i + 1) % count) for i in range(count)]
    down = [(j, i) for i, j in up]
    first = lax.ppermute(part, ZH, up)
    third = lax.ppermute(part, ZH, down)
    second = lax.ppermute(first, ZH, up)
    turned = jnp.stack([third, second, first, part] * 2)
    return lax.dynamic_slice_in_dim(turned, count - 1 - place, count, 0)


def other_core(value):
    return lax.ppermute(value, CORE, [(0, 1), (1, 0)])


def both_cores(mine):
    theirs = other_core(mine)
    first = lax.axis_index(CORE) == 0
    return jnp.stack([jnp.where(first, mine, theirs), jnp.where(first, theirs, mine)])


def plane_gather(piece):
    count = lax.axis_size(PLANE)
    copies = jnp.broadcast_to(piece[None], (count,) + piece.shape)
    return lax.all_to_all(copies, PLANE, 0, 0, tiled=True)


def gathered_weights(norm_gain, w_query, w_key, w_value, w_out):
    nx, ny, nz = (lax.axis_size(X), lax.axis_size(Y), lax.axis_size(ZH))
    depth, hidden_width = w_query.shape
    out_depth, model_width = w_out.shape
    rows = depth // (nx * ny)
    out_rows, out_columns = (out_depth // nx, model_width // ny)
    folds = out_rows // rows
    part = own_slices(norm_gain, w_query, w_key, w_value, w_out, rows, out_rows, out_columns)
    part = column_gather(part)
    width = 3 * hidden_width + folds * out_columns
    gain = both_cores(part[:, :, width:])[:, :, 0]
    gain = jnp.swapaxes(gain, 0, 1).reshape(-1)
    whole = plane_gather(part[:, :, :width])
    whole = both_cores(whole)
    joint = jnp.transpose(whole[..., : 3 * hidden_width], (2, 0, 1, 3, 4))
    joint = joint.reshape(2 * nz * depth, 3 * hidden_width)
    whole = whole.reshape(2, nx, ny, nz, rows, width)
    bands = []
    for i in range(folds):
        begin = 3 * hidden_width + i * out_columns
        bands.append(jnp.transpose(whole[..., begin : begin + out_columns], (2, 3, 0, 1, 4, 5)))
    bands = jnp.stack(bands, axis=4).reshape(ny, 2 * nz * out_depth, out_columns)
    out_whole = jnp.concatenate([bands[i] for i in range(ny)], axis=1)
    return gain, joint, out_whole


def halved_gradient(attended, cotangent):
    nz = lax.axis_size(ZH)
    partial = jnp.einsum("sre,sru->eu", attended, cotangent, preferred_element_type=F32)
    width, model_width = partial.shape
    partial = partial.reshape(nz, 2, width // (2 * nz), model_width)
    first = lax.axis_index(CORE) == 0
    kept = jnp.where(first, partial[:, 0], partial[:, 1])
    sent = jnp.where(first, partial[:, 1], partial[:, 0])
    return (kept + other_core(sent)).astype(BF16)


def summed_gradient(half, total_samples):
    nx, ny, nz, nl = (lax.axis_size(X), lax.axis_size(Y), lax.axis_size(ZH), lax.axis_size(ZL))
    _, share, model_width = half.shape
    rows, columns = (share // nx, model_width // ny)
    half = jnp.stack([half[:, :, i * columns : (i + 1) * columns] for i in range(ny)])
    half = jnp.swapaxes(half.reshape(ny, nz, nx, rows, columns), 1, 2)
    half = half.reshape(ny * nx, nz, rows, columns)
    half = lax.all_to_all(half, (Y, X), 0, 0, tiled=True)
    part = jnp.sum(half.astype(F32), axis=0)
    part = jnp.broadcast_to(part[None], (nl, nz, rows, columns)).reshape(nl * nz, rows, columns)
    part = lax.all_to_all(part, COLUMN, 0, 0, tiled=True)
    part = jnp.sum(part, axis=0) / total_samples
    whole = plane_gather(part).reshape(nx, ny, rows, columns)
    return jnp.concatenate([whole[:, i].reshape(share, columns) for i in range(ny)], axis=1)


def shards(
    inputs, norm_gain, w_query, w_key, w_value, w_out, neighbors, slot_valid, output_cotangent
):
    samples, length, _ = inputs.shape
    block_count, _ = neighbors.shape
    block_len = length // block_count
    window_blocks = 3 * block_count
    groups = lax.axis_size(DOMAIN)
    up = [(i, i + 1) for i in range(groups - 1)]
    down = [(j, i) for i, j in up]
    below = lax.ppermute(inputs, DOMAIN, up)
    above = lax.ppermute(inputs, DOMAIN, down)
    gain, w_joint, w_full_out = gathered_weights(norm_gain, w_query, w_key, w_value, w_out)
    gain_float = gain.astype(F32)

    def inverse_of(rows):
        rows = rows.astype(F32)
        return lax.rsqrt(jnp.mean(rows * rows, axis=-1, keepdims=True) + EPSILON)

    inverse_rms = inverse_of(inputs)
    window = jnp.concatenate([below, inputs, above], axis=1)
    normed = (window.astype(F32) * inverse_of(window) * gain_float).astype(BF16)
    joint = jnp.einsum("sti,iy->sty", normed, w_joint, preferred_element_type=F32).astype(BF16)
    d_attention = jnp.einsum(
        "stz,yz->sty", output_cotangent, w_full_out, preferred_element_type=F32
    ).astype(BF16)

    group = lax.axis_index(DOMAIN)
    local_index = neighbors - (group - 1) * block_count
    matches = jnp.logical_and(
        local_index[:, :, None] == jnp.arange(window_blocks, dtype=jnp.int32)[None, None, :],
        (slot_valid > 0)[:, :, None],
    )
    bias = jnp.where(jnp.any(matches, axis=1).T, 0.0, MASKED).astype(F32)
    bias = jnp.tile(jnp.repeat(bias, block_len, axis=1), (1, 2))[:, None, :]

    attended, stats = forward_attention(bias, joint)
    half = halved_gradient(attended, output_cotangent)
    half, d_attention = lax.optimization_barrier((half, d_attention))
    members = lax.axis_size(MEMBER)
    grad_wout = summed_gradient(half, samples * members)
    grads = (lax.ppermute(d_attention, DOMAIN, up), lax.ppermute(d_attention, DOMAIN, down))
    d_query, own, stats = query_gradient(bias, joint, d_attention, stats)
    shape, flat = (stats.shape, (-1, stats.shape[-1]))
    stats, attended = lax.optimization_barrier((stats, attended))

    def message(third):
        rows = bias[third * block_count : (third + 1) * block_count]
        return jnp.concatenate([stats.reshape(flat), rows.reshape(flat)], axis=0)

    received = (
        lax.ppermute(message(2), DOMAIN, up),
        lax.ppermute(message(0), DOMAIN, down),
    )
    attn_out = jnp.einsum(
        "sty,yb->stb", attended, w_full_out, preferred_element_type=F32
    ).astype(BF16)
    side_stats = [rows[:-block_count].reshape(shape) for rows in received]
    side_bias = [rows[-block_count:][:, None, :] for rows in received]
    d_key, d_value = key_gradient(side_bias, joint, grads, side_stats, own)
    d_joint = jnp.concatenate([d_query, d_key, d_value], axis=-1)
    d_normed = jnp.einsum("sty,iy->sti", d_joint, w_joint, preferred_element_type=F32)
    inputs_float = inputs.astype(F32)
    scaled = d_normed * gain_float
    inner = jnp.mean(scaled * inputs_float, axis=-1, keepdims=True)
    d_input = inverse_rms * scaled - inputs_float * inverse_rms**3 * inner
    return attn_out, d_input.astype(BF16), grad_wout


def solution(mesh):
    fine = Mesh(mesh.devices.reshape(4, 4, 4, 4, 2), (X, Y, ZL, ZH, CORE))
    placed = (
        P(MEMBER, DOMAIN, None),
        P(MEMBER),
        P(MEMBER, None),
        P(MEMBER, None),
        P(MEMBER, None),
        P(MEMBER, None),
        P(DOMAIN, None),
        P(DOMAIN, None),
        P(MEMBER, DOMAIN, None),
    )

    return jax.shard_map(
        shards,
        mesh=fine,
        in_specs=placed,
        out_specs=(P(MEMBER, DOMAIN, None), P(MEMBER, DOMAIN, None), P(MEMBER, None)),
        check_vma=False,
    )
```

```python
import jax
import jax.numpy as jnp
from jax import lax
from jax.experimental import pallas as pl
from jax.experimental.pallas import tpu as pltpu
from jax.sharding import Mesh
from jax.sharding import PartitionSpec as P


HEAD_DIM = 64
PAIR = 2 * HEAD_DIM
SCALE = HEAD_DIM**-0.5
EPSILON = 1e-06
MASKED = -1e30
X, Y, ZL, ZH, CORE = "x", "y", "zl", "zh", "core"
DOMAIN = (X, Y, ZL)
MEMBER = (ZH, CORE)
PLANE = (X, Y)
COLUMN = (ZL, ZH)
BF16, F32 = jnp.bfloat16, jnp.float32


def contract(a, b, da, db):
    return lax.dot_general(a, b, (((da,), (db,)), ((), ())), preferred_element_type=F32)


def head_lanes():
    return lax.broadcasted_iota(jnp.int32, (1, PAIR), 1) < HEAD_DIM


def stacked(both, scale=1.0):
    near = head_lanes()
    both = both * jnp.asarray(scale, both.dtype)
    zero = jnp.zeros_like(both)
    return jnp.concatenate([jnp.where(near, both, zero), jnp.where(near, zero, both)], axis=0)


def merged(columns):
    both = columns.T
    rows = both.shape[0] // 2
    return jnp.where(head_lanes(), both[:rows], both[rows:])


def masked_scores(bias, key, query):
    blocks = bias.shape[0]
    span, columns = (key.shape[0], query.shape[0])
    scores = contract(key, query, 1, 1).reshape(blocks, span // blocks, columns)
    return (scores + bias).reshape(span, columns)


def forward_kernel(bias_ref, q_ref, k_ref, v_ref, att_ref, stat_ref):
    scores = masked_scores(bias_ref[...], k_ref[0], stacked(q_ref[0], SCALE))
    row_max = jnp.max(scores, axis=0, keepdims=True)
    shifted = jnp.exp(scores - row_max)
    total = jnp.sum(shifted, axis=0, keepdims=True)
    prob_bf = (shifted * (1.0 / total)).astype(BF16)
    att_ref[0] = merged(contract(v_ref[0], prob_bf, 0, 0)).astype(BF16)
    stat_ref[0, 0] = row_max + jnp.log(total)


def probability(bias, key, query, stats):
    return jnp.exp(masked_scores(bias, key, query) - stats[0:1])


def query_kernel(bias_ref, q_ref, k_ref, v_ref, g_ref, stat_ref, dq_ref, own_ref, sent_ref):
    rows = q_ref.shape[1]
    query, key, value, grad = (stacked(q_ref[0], SCALE), k_ref[0], v_ref[0], stacked(g_ref[0]))
    stats = stat_ref[0, 0]
    prob = probability(bias_ref[...], key, query, stats)
    d_prob = contract(value, grad, 1, 1)
    delta = jnp.sum(prob * d_prob, axis=0, keepdims=True)
    d_score = (prob * (d_prob - delta)).astype(BF16)
    dq_ref[0] = (merged(contract(key, d_score, 0, 0)) * SCALE).astype(BF16)
    own_ref[0, 0] = contract(d_score[rows : 2 * rows], query, 1, 0)
    own_ref[1, 0] = contract(prob[rows : 2 * rows].astype(BF16), grad, 1, 0)
    third = bias_ref.shape[0] // 3
    sent_ref[0, 0, 0:1, :] = stats
    sent_ref[0, 0, 1:2, :] = delta
    for i in range(third):
        sent_ref[0, 0, 2 + i : 3 + i, :] = bias_ref[2 * third + i]
        sent_ref[0, 0, 2 + third + i : 3 + third + i, :] = bias_ref[i]


def key_kernel(
    low_q_ref,
    high_q_ref,
    k_ref,
    v_ref,
    low_g_ref,
    high_g_ref,
    low_stat_ref,
    high_stat_ref,
    own_ref,
    dk_ref,
    dv_ref,
):
    key, value = (k_ref[0], v_ref[0])
    d_key, d_value = (own_ref[0, 0], own_ref[1, 0])
    sides = ((low_q_ref, low_g_ref, low_stat_ref), (high_q_ref, high_g_ref, high_stat_ref))
    for side, (q_ref, g_ref, stat_ref) in enumerate(sides):
        query, grad, stats = (stacked(q_ref[0], SCALE), stacked(g_ref[0]), stat_ref[0, 0])
        third = (stats.shape[0] - 2) // 2
        first = 2 + side * third
        bias = jnp.stack([stats[first + i : first + i + 1] for i in range(third)])
        prob = probability(bias, key, query, stats)
        d_score = (prob * (contract(value, grad, 1, 1) - stats[1:2])).astype(BF16)
        d_key += contract(d_score, query, 1, 0).astype(BF16).astype(F32)
        d_value += contract(prob.astype(BF16), grad, 1, 0).astype(BF16).astype(F32)
    dk_ref[0] = d_key.astype(BF16)
    dv_ref[0] = d_value.astype(BF16)


class Plan:
    def __init__(self, joint):
        samples, span, width = joint.shape
        self.rows, self.width, self.span = (span // 3, width // 3, span)
        self.samples, self.pairs = (samples, width // 3 // PAIR)
        self.grid = (samples, self.pairs)
        self.narrow = pl.BlockSpec((1, self.rows, PAIR), lambda s, h: (s, 0, h))
        self.split = pl.BlockSpec((2, 1, self.rows, PAIR), lambda s, h: (0, s, 0, h))

    def joint(self, kind, third=None):
        first = kind * self.pairs
        if third is None:
            return pl.BlockSpec((1, self.span, PAIR), lambda s, h: (s, 0, h + first))
        return pl.BlockSpec((1, self.rows, PAIR), lambda s, h: (s, third, h + first))

    def bias(self, bias):
        return pl.BlockSpec(bias.shape, lambda s, h: (0, 0, 0))

    def stat(self, count):
        return pl.BlockSpec((1, 1, count, 2 * self.rows), lambda s, h: (s, h, 0, 0))

    def stat_shape(self, count):
        return jax.ShapeDtypeStruct((self.samples, self.pairs, count, 2 * self.rows), F32)

    def narrow_shape(self):
        return jax.ShapeDtypeStruct((self.samples, self.rows, self.width), BF16)

    def call(self, kernel, products, in_specs, out_specs, out_shape):
        work = self.samples * self.rows * self.span * self.width
        return pl.pallas_call(
            kernel,
            grid=self.grid,
            in_specs=in_specs,
            out_specs=out_specs,
            out_shape=out_shape,
            cost_estimate=pl.CostEstimate(
                flops=2 * products * work,
                transcendentals=work // HEAD_DIM,
                bytes_accessed=3 * products * self.samples * self.rows * self.width,
            ),
            compiler_params=pltpu.CompilerParams(vmem_limit_bytes=16 * 2**20),
        )


def forward_attention(bias, joint):
    plan = Plan(joint)
    given = [plan.bias(bias), plan.joint(0, 1), plan.joint(1), plan.joint(2)]
    outs = ([plan.narrow, plan.stat(1)], [plan.narrow_shape(), plan.stat_shape(1)])
    return plan.call(forward_kernel, 2, given, *outs)(bias, joint, joint, joint)


def query_gradient(bias, joint, grad, stats):
    plan = Plan(joint)
    count = 2 + 2 * (bias.shape[0] // 3)
    given = [plan.bias(bias), plan.joint(0, 1), plan.joint(1), plan.joint(2)]
    given += [plan.narrow, plan.stat(1)]
    own = jax.ShapeDtypeStruct((2, plan.samples, plan.rows, plan.width), F32)
    outs = (
        [plan.narrow, plan.split, plan.stat(count)],
        [plan.narrow_shape(), own, plan.stat_shape(count)],
    )
    return plan.call(query_kernel, 4, given, *outs)(bias, joint, joint, joint, grad, stats)


def key_gradient(joint, grads, stats, own):
    plan = Plan(joint)
    given = [plan.joint(0, 0), plan.joint(0, 2), plan.joint(1, 1), plan.joint(2, 1)]
    given += [plan.narrow] * 2 + [plan.stat(stats[0].shape[2])] * 2 + [plan.split]
    outs = ([plan.narrow] * 2, [plan.narrow_shape()] * 2)
    call = plan.call(key_kernel, 3, given, *outs)
    return call(joint, joint, joint, joint, *grads, *stats, own)


def slice_kernel(place_ref, q_ref, k_ref, v_ref, out_ref, gain_ref, part_ref):
    rows, width = q_ref.shape
    columns = out_ref.shape[1]
    folds = out_ref.shape[0] // rows
    for i, ref in enumerate((q_ref, k_ref, v_ref)):
        part_ref[:, i * width : (i + 1) * width] = ref[...]
    for i in range(folds):
        begin = 3 * width + i * columns
        part_ref[:, begin : begin + columns] = out_ref[i * rows : (i + 1) * rows, :]
    begin = 3 * width + folds * columns
    part_ref[:, begin:] = jnp.broadcast_to(gain_ref[...], (rows, gain_ref.shape[1]))


def own_slices(norm_gain, w_query, w_key, w_value, w_out, rows, out_rows, out_columns):
    depth, width = w_query.shape
    xi, yi = (lax.axis_index(X), lax.axis_index(Y))
    place = jnp.stack([xi * lax.axis_size(Y) + yi, xi, yi])
    band = pl.BlockSpec((rows, width), lambda i, place: (place[0], 0))
    total = 3 * width + out_rows // rows * out_columns + depth
    return pl.pallas_call(
        slice_kernel,
        grid_spec=pltpu.PrefetchScalarGridSpec(
            num_scalar_prefetch=1,
            grid=(1,),
            in_specs=[
                band,
                band,
                band,
                pl.BlockSpec((out_rows, out_columns), lambda i, place: (place[1], place[2])),
                pl.BlockSpec((1, depth), lambda i, place: (0, 0)),
            ],
            out_specs=pl.BlockSpec((rows, total), lambda i, place: (0, 0)),
        ),
        out_shape=jax.ShapeDtypeStruct((rows, total), BF16),
    )(place, w_query, w_key, w_value, w_out, norm_gain[None])


def column_gather(part):
    count = lax.axis_size(ZH)
    up = [(i, (i + 1) % count) for i in range(count)]
    down = [(j, i) for i, j in up]
    first = lax.ppermute(part, ZH, up)
    third = lax.ppermute(part, ZH, down)
    second = lax.ppermute(first, ZH, up)
    return jnp.stack([first, third, second])


def other_core(value):
    return lax.ppermute(value, CORE, [(0, 1), (1, 0)])


def plane_gather(piece):
    count = lax.axis_size(PLANE)
    copies = jnp.broadcast_to(piece[None], (count,) + piece.shape)
    return lax.all_to_all(copies, PLANE, 0, 0, tiled=True)


def pack_kernel(q_ref, k_ref, v_ref, out_ref, gain_ref, mine_ref):
    depth, width = q_ref.shape
    out_depth, half = (out_ref.shape[0], out_ref.shape[1] // 2)
    for i, ref in enumerate((q_ref, k_ref, v_ref)):
        mine_ref[:, i * width : (i + 1) * width] = ref[...]
    begin = 3 * width
    mine_ref[:out_depth, begin : begin + half] = out_ref[:, :half]
    mine_ref[out_depth:, begin : begin + half] = out_ref[:, half:]
    mine_ref[:, begin + half :] = jnp.broadcast_to(gain_ref[...], (depth, gain_ref.shape[1]))


def assembly_kernel(
    place_ref, mine_ref, theirs_ref, far_ref, other_ref, joint_ref, out_ref, gain_ref
):
    step = pl.program_id(0)
    width = joint_ref.shape[1]
    half = out_ref.shape[1] // 2
    depth, rows = (out_ref.shape[0], gain_ref.shape[1])
    count = far_ref.shape[0]
    columns = (far_ref.shape[3] - width - gain_ref.shape[2]) // 2
    across = out_ref.shape[1] // columns

    def near(ref):
        joint_ref[...] = ref[:, :width]
        out_ref[:, :half] = ref[:depth, width : width + half]
        out_ref[:, half:] = ref[depth:, width : width + half]
        gain_ref[0] = ref[:rows, width + half :]

    def distant(ref):
        for s in range(count):
            joint_ref[s * rows : (s + 1) * rows, :] = ref[s, 0, :, :width]
            top, left = (s // across * 2 * rows, s % across * columns)
            for fold in range(2):
                begin = width + fold * columns
                place = slice(top + fold * rows, top + (fold + 1) * rows)
                out_ref[place, left : left + columns] = ref[s, 0, :, begin : begin + columns]
        gain_ref[0] = ref[0, 0, :, width + 2 * columns :]

    pl.when(step == 0)(lambda: near(mine_ref))
    pl.when(step == 1)(lambda: near(theirs_ref))
    pl.when(jnp.logical_and(step > 1, step < 5))(lambda: distant(far_ref))
    pl.when(step >= 5)(lambda: distant(other_ref))


def assembled_weights(mine, theirs, far, other, width, out_shape):
    nz = lax.axis_size(ZH)
    zh, core = (lax.axis_index(ZH), lax.axis_index(CORE))
    peers = [zh, (zh + nz - 1) % nz, (zh + 1) % nz, (zh + 2) % nz]
    same = [2 * peer + core for peer in peers]
    swapped = [2 * peer + 1 - core for peer in peers]
    place = jnp.stack([same[0], swapped[0]] + same[1:] + swapped[1:])
    count, _, rows, total = far.shape
    depth = mine.shape[0]
    out_depth, model_width = out_shape
    gain_width = total - width - model_width // 2
    whole = pl.BlockSpec(mine.shape, lambda i, place: (0, 0))

    def distant(first):
        return pl.BlockSpec(
            (count, 1, rows, total),
            lambda i, place: (0, jnp.clip(i - first, 0, 2), 0, 0),
        )

    shape = jax.ShapeDtypeStruct
    return pl.pallas_call(
        assembly_kernel,
        grid_spec=pltpu.PrefetchScalarGridSpec(
            num_scalar_prefetch=1,
            grid=(2 * nz,),
            in_specs=[whole, whole, distant(2), distant(5)],
            out_specs=[
                pl.BlockSpec((depth, width), lambda i, place: (place[i], 0)),
                pl.BlockSpec((out_depth, model_width), lambda i, place: (place[i], 0)),
                pl.BlockSpec((1, rows, gain_width), lambda i, place: (place[i], 0, 0)),
            ],
        ),
        out_shape=[
            shape((2 * nz * depth, width), BF16),
            shape((2 * nz * out_depth, model_width), BF16),
            shape((2 * nz, rows, gain_width), BF16),
        ],
        cost_estimate=pl.CostEstimate(flops=0, transcendentals=0, bytes_accessed=2**23),
    )(place, mine, theirs, far, other)


def gathered_weights(norm_gain, w_query, w_key, w_value, w_out):
    nx, ny = (lax.axis_size(X), lax.axis_size(Y))
    depth, hidden_width = w_query.shape
    out_depth, model_width = w_out.shape
    rows = depth // (nx * ny)
    out_rows, out_columns = (out_depth // nx, model_width // ny)
    part = own_slices(norm_gain, w_query, w_key, w_value, w_out, rows, out_rows, out_columns)
    part = column_gather(part)
    half = model_width // 2
    far = plane_gather(part)
    mine = pl.pallas_call(
        pack_kernel,
        out_shape=jax.ShapeDtypeStruct((depth, 3 * hidden_width + half + depth), BF16),
    )(w_query, w_key, w_value, w_out, norm_gain[None])
    theirs = other_core(mine)
    other = other_core(far)
    joint, out_whole, gain = assembled_weights(
        mine, theirs, far, other, 3 * hidden_width, w_out.shape
    )
    return gain[:, 0, :].reshape(-1), joint, out_whole


def halved_gradient(attended, cotangent):
    nz = lax.axis_size(ZH)
    partial = jnp.einsum("sre,sru->eu", attended, cotangent, preferred_element_type=F32)
    width, model_width = partial.shape
    partial = partial.reshape(nz, 2, width // (2 * nz), model_width)
    first = lax.axis_index(CORE) == 0
    kept = jnp.where(first, partial[:, 0], partial[:, 1])
    sent = jnp.where(first, partial[:, 1], partial[:, 0])
    return (kept + other_core(sent)).astype(BF16)


def summed_gradient(half, total_samples):
    nx, ny, nz, nl = (lax.axis_size(X), lax.axis_size(Y), lax.axis_size(ZH), lax.axis_size(ZL))
    _, share, model_width = half.shape
    rows, columns = (share // nx, model_width // ny)
    half = jnp.stack([half[:, :, i * columns : (i + 1) * columns] for i in range(ny)])
    half = jnp.swapaxes(half.reshape(ny, nz, nx, rows, columns), 1, 2)
    half = half.reshape(ny * nx, nz, rows, columns)
    half = lax.all_to_all(half, (Y, X), 0, 0, tiled=True)
    part = jnp.sum(half.astype(F32), axis=0)
    part = jnp.broadcast_to(part[None], (nl, nz, rows, columns)).reshape(nl * nz, rows, columns)
    part = lax.all_to_all(part, COLUMN, 0, 0, tiled=True)
    part = jnp.sum(part, axis=0) / total_samples
    whole = plane_gather(part).reshape(nx, ny, rows, columns)
    return jnp.concatenate([whole[:, i].reshape(share, columns) for i in range(ny)], axis=1)


def shards(
    inputs, norm_gain, w_query, w_key, w_value, w_out, neighbors, slot_valid, output_cotangent
):
    samples, length, _ = inputs.shape
    block_count, _ = neighbors.shape
    block_len = length // block_count
    window_blocks = 3 * block_count
    groups = lax.axis_size(DOMAIN)
    up = [(i, i + 1) for i in range(groups - 1)]
    down = [(j, i) for i, j in up]
    below = lax.ppermute(inputs, DOMAIN, up)
    above = lax.ppermute(inputs, DOMAIN, down)
    gain, w_joint, w_full_out = gathered_weights(norm_gain, w_query, w_key, w_value, w_out)
    gain_float = gain.astype(F32)

    def inverse_of(rows):
        rows = rows.astype(F32)
        return lax.rsqrt(jnp.mean(rows * rows, axis=-1, keepdims=True) + EPSILON)

    inverse_rms = inverse_of(inputs)
    window = jnp.concatenate([below, inputs, above], axis=1)
    normed = (window.astype(F32) * inverse_of(window) * gain_float).astype(BF16)
    joint = jnp.einsum("sti,iy->sty", normed, w_joint, preferred_element_type=F32).astype(BF16)
    joint = pltpu.with_memory_space_constraint(joint, pltpu.HBM)
    d_attention = jnp.einsum(
        "stz,yz->sty", output_cotangent, w_full_out, preferred_element_type=F32
    ).astype(BF16)

    group = lax.axis_index(DOMAIN)
    local_index = neighbors - (group - 1) * block_count
    matches = jnp.logical_and(
        local_index[:, :, None] == jnp.arange(window_blocks, dtype=jnp.int32)[None, None, :],
        (slot_valid > 0)[:, :, None],
    )
    bias = jnp.where(jnp.any(matches, axis=1).T, 0.0, MASKED).astype(F32)
    bias = jnp.tile(jnp.repeat(bias, block_len, axis=1), (1, 2))[:, None, :]

    grads = (lax.ppermute(d_attention, DOMAIN, up), lax.ppermute(d_attention, DOMAIN, down))
    attended, stats = forward_attention(bias, joint)
    half = halved_gradient(attended, output_cotangent)
    members = lax.axis_size(MEMBER)
    grad_wout = summed_gradient(half, samples * members)
    d_query, own, stats = query_gradient(bias, joint, d_attention, stats)
    side_stats = (lax.ppermute(stats, DOMAIN, up), lax.ppermute(stats, DOMAIN, down))
    d_key, d_value = key_gradient(joint, grads, side_stats, own)
    attn_out = jnp.einsum(
        "sty,yb->stb", attended, w_full_out, preferred_element_type=F32
    ).astype(BF16)
    d_joint = jnp.concatenate([d_query, d_key, d_value], axis=-1)
    d_normed = jnp.einsum("sty,iy->sti", d_joint, w_joint, preferred_element_type=F32)
    inputs_float = inputs.astype(F32)
    scaled = d_normed * gain_float
    inner = jnp.mean(scaled * inputs_float, axis=-1, keepdims=True)
    d_input = inverse_rms * scaled - inputs_float * inverse_rms**3 * inner
    return attn_out, d_input.astype(BF16), grad_wout


def solution(mesh):
    fine = Mesh(mesh.devices.reshape(4, 4, 4, 4, 2), (X, Y, ZL, ZH, CORE))
    placed = (
        P(MEMBER, DOMAIN, None),
        P(MEMBER),
        P(MEMBER, None),
        P(MEMBER, None),
        P(MEMBER, None),
        P(MEMBER, None),
        P(DOMAIN, None),
        P(DOMAIN, None),
        P(MEMBER, DOMAIN, None),
    )

    return jax.shard_map(
        shards,
        mesh=fine,
        in_specs=placed,
        out_specs=(P(MEMBER, DOMAIN, None), P(MEMBER, DOMAIN, None), P(MEMBER, None)),
        check_vma=False,
    )
```

```python
import jax
import jax.numpy as jnp
from jax import lax
from jax.experimental import pallas as pl
from jax.experimental.pallas import tpu as pltpu
from jax.sharding import Mesh
from jax.sharding import PartitionSpec as P


HEAD_DIM = 64
PAIR = 2 * HEAD_DIM
SCALE = HEAD_DIM**-0.5
EPSILON = 1e-06
MASKED = -1e30
X, Y, ZL, ZH, CORE = "x", "y", "zl", "zh", "core"
DOMAIN = (X, Y, ZL)
MEMBER = (ZH, CORE)
PLANE = (X, Y)
COLUMN = (ZL, ZH)
BF16, F32 = jnp.bfloat16, jnp.float32


def contract(a, b, da, db):
    return lax.dot_general(a, b, (((da,), (db,)), ((), ())), preferred_element_type=F32)


def head_lanes():
    return lax.broadcasted_iota(jnp.int32, (1, PAIR), 1) < HEAD_DIM


def stacked(both, scale=1.0):
    near = head_lanes()
    both = both * jnp.asarray(scale, both.dtype)
    zero = jnp.zeros_like(both)
    return jnp.concatenate([jnp.where(near, both, zero), jnp.where(near, zero, both)], axis=0)


def merged(columns):
    both = columns.T
    rows = both.shape[0] // 2
    return jnp.where(head_lanes(), both[:rows], both[rows:])


def masked_scores(bias, key, query):
    blocks = bias.shape[0]
    span, columns = (key.shape[0], query.shape[0])
    scores = contract(key, query, 1, 1).reshape(blocks, span // blocks, columns)
    return (scores + bias).reshape(span, columns)


def forward_kernel(bias_ref, q_ref, k_ref, v_ref, att_ref, stat_ref):
    scores = masked_scores(bias_ref[...], k_ref[0], stacked(q_ref[0], SCALE))
    row_max = jnp.max(scores, axis=0, keepdims=True)
    shifted = jnp.exp(scores - row_max)
    total = jnp.sum(shifted, axis=0, keepdims=True)
    prob_bf = (shifted * (1.0 / total)).astype(BF16)
    att_ref[0] = merged(contract(v_ref[0], prob_bf, 0, 0)).astype(BF16)
    stat_ref[0, 0] = row_max + jnp.log(total)


def probability(bias, key, query, stats):
    return jnp.exp(masked_scores(bias, key, query) - stats[0:1])


def query_kernel(bias_ref, q_ref, k_ref, v_ref, g_ref, stat_ref, dq_ref, own_ref, sent_ref):
    rows = q_ref.shape[1]
    query, key, value, grad = (stacked(q_ref[0], SCALE), k_ref[0], v_ref[0], stacked(g_ref[0]))
    stats = stat_ref[0, 0]
    prob = probability(bias_ref[...], key, query, stats)
    d_prob = contract(value, grad, 1, 1)
    delta = jnp.sum(prob * d_prob, axis=0, keepdims=True)
    d_score = (prob * (d_prob - delta)).astype(BF16)
    dq_ref[0] = (merged(contract(key, d_score, 0, 0)) * SCALE).astype(BF16)
    own_ref[0, 0] = contract(d_score[rows : 2 * rows], query, 1, 0)
    own_ref[1, 0] = contract(prob[rows : 2 * rows].astype(BF16), grad, 1, 0)
    third = bias_ref.shape[0] // 3
    sent_ref[0, 0, 0:1, :] = stats
    sent_ref[0, 0, 1:2, :] = delta
    for i in range(third):
        sent_ref[0, 0, 2 + i : 3 + i, :] = bias_ref[2 * third + i]
        sent_ref[0, 0, 2 + third + i : 3 + third + i, :] = bias_ref[i]


def key_kernel(
    low_q_ref,
    high_q_ref,
    k_ref,
    v_ref,
    low_g_ref,
    high_g_ref,
    low_stat_ref,
    high_stat_ref,
    own_ref,
    dk_ref,
    dv_ref,
):
    key, value = (k_ref[0], v_ref[0])
    d_key, d_value = (own_ref[0, 0], own_ref[1, 0])
    sides = ((low_q_ref, low_g_ref, low_stat_ref), (high_q_ref, high_g_ref, high_stat_ref))
    for side, (q_ref, g_ref, stat_ref) in enumerate(sides):
        query, grad, stats = (stacked(q_ref[0], SCALE), stacked(g_ref[0]), stat_ref[0, 0])
        third = (stats.shape[0] - 2) // 2
        first = 2 + side * third
        bias = jnp.stack([stats[first + i : first + i + 1] for i in range(third)])
        prob = probability(bias, key, query, stats)
        d_score = (prob * (contract(value, grad, 1, 1) - stats[1:2])).astype(BF16)
        d_key += contract(d_score, query, 1, 0).astype(BF16).astype(F32)
        d_value += contract(prob.astype(BF16), grad, 1, 0).astype(BF16).astype(F32)
    dk_ref[0] = d_key.astype(BF16)
    dv_ref[0] = d_value.astype(BF16)


class Plan:
    def __init__(self, joint):
        samples, span, width = joint.shape
        self.rows, self.width, self.span = (span // 3, width // 3, span)
        self.samples, self.pairs = (samples, width // 3 // PAIR)
        self.grid = (samples, self.pairs)
        self.narrow = pl.BlockSpec((1, self.rows, PAIR), lambda s, h: (s, 0, h))
        self.split = pl.BlockSpec((2, 1, self.rows, PAIR), lambda s, h: (0, s, 0, h))

    def joint(self, kind, third=None):
        first = kind * self.pairs
        if third is None:
            return pl.BlockSpec((1, self.span, PAIR), lambda s, h: (s, 0, h + first))
        return pl.BlockSpec((1, self.rows, PAIR), lambda s, h: (s, third, h + first))

    def bias(self, bias):
        return pl.BlockSpec(bias.shape, lambda s, h: (0, 0, 0))

    def stat(self, count):
        return pl.BlockSpec((1, 1, count, 2 * self.rows), lambda s, h: (s, h, 0, 0))

    def stat_shape(self, count):
        return jax.ShapeDtypeStruct((self.samples, self.pairs, count, 2 * self.rows), F32)

    def narrow_shape(self):
        return jax.ShapeDtypeStruct((self.samples, self.rows, self.width), BF16)

    def call(self, kernel, products, in_specs, out_specs, out_shape):
        work = self.samples * self.rows * self.span * self.width
        return pl.pallas_call(
            kernel,
            grid=self.grid,
            in_specs=in_specs,
            out_specs=out_specs,
            out_shape=out_shape,
            cost_estimate=pl.CostEstimate(
                flops=2 * products * work,
                transcendentals=work // HEAD_DIM,
                bytes_accessed=3 * products * self.samples * self.rows * self.width,
            ),
            compiler_params=pltpu.CompilerParams(vmem_limit_bytes=16 * 2**20),
        )


def forward_attention(bias, joint):
    plan = Plan(joint)
    given = [plan.bias(bias), plan.joint(0, 1), plan.joint(1), plan.joint(2)]
    outs = ([plan.narrow, plan.stat(1)], [plan.narrow_shape(), plan.stat_shape(1)])
    return plan.call(forward_kernel, 2, given, *outs)(bias, joint, joint, joint)


def query_gradient(bias, joint, grad, stats):
    plan = Plan(joint)
    count = 2 + 2 * (bias.shape[0] // 3)
    given = [plan.bias(bias), plan.joint(0, 1), plan.joint(1), plan.joint(2)]
    given += [plan.narrow, plan.stat(1)]
    own = jax.ShapeDtypeStruct((2, plan.samples, plan.rows, plan.width), F32)
    outs = (
        [plan.narrow, plan.split, plan.stat(count)],
        [plan.narrow_shape(), own, plan.stat_shape(count)],
    )
    return plan.call(query_kernel, 4, given, *outs)(bias, joint, joint, joint, grad, stats)


def key_gradient(joint, grads, stats, own):
    plan = Plan(joint)
    given = [plan.joint(0, 0), plan.joint(0, 2), plan.joint(1, 1), plan.joint(2, 1)]
    given += [plan.narrow] * 2 + [plan.stat(stats[0].shape[2])] * 2 + [plan.split]
    outs = ([plan.narrow] * 2, [plan.narrow_shape()] * 2)
    call = plan.call(key_kernel, 3, given, *outs)
    return call(joint, joint, joint, joint, *grads, *stats, own)


def slice_kernel(place_ref, q_ref, k_ref, v_ref, out_ref, gain_ref, part_ref):
    rows, width = q_ref.shape
    half = width // 2
    columns = out_ref.shape[1]

    @pl.when(place_ref[1] == 0)
    def _():
        part_ref[:, :width] = q_ref[...]
        part_ref[:, width : width + half] = k_ref[:, :half]

    @pl.when(place_ref[1] != 0)
    def _():
        part_ref[:, :half] = k_ref[:, half:]
        part_ref[:, half : half + width] = v_ref[...]

    begin = width + half
    part_ref[:, begin : begin + columns] = out_ref[...]
    part_ref[:, begin + columns :] = jnp.broadcast_to(gain_ref[...], (rows, gain_ref.shape[1]))


def own_slices(norm_gain, w_query, w_key, w_value, w_out):
    nx, ny = (lax.axis_size(X), lax.axis_size(Y))
    xi, yi = (lax.axis_index(X), lax.axis_index(Y))
    depth, width = w_query.shape
    rows, columns = (w_out.shape[0] // nx, w_out.shape[1] // ny)
    number = xi * ny + yi
    place = jnp.stack([number // 2, number % 2, xi, yi])
    band = pl.BlockSpec((rows, width), lambda i, place: (place[0], 0))
    total = width + width // 2 + columns + depth
    return pl.pallas_call(
        slice_kernel,
        grid_spec=pltpu.PrefetchScalarGridSpec(
            num_scalar_prefetch=1,
            grid=(1,),
            in_specs=[
                band,
                band,
                band,
                pl.BlockSpec((rows, columns), lambda i, place: (place[2], place[3])),
                pl.BlockSpec((1, depth), lambda i, place: (0, 0)),
            ],
            out_specs=pl.BlockSpec((rows, total), lambda i, place: (0, 0)),
        ),
        out_shape=jax.ShapeDtypeStruct((rows, total), BF16),
    )(place, w_query, w_key, w_value, w_out, norm_gain[None])


def column_gather(part):
    count = lax.axis_size(ZH)
    up = [(i, (i + 1) % count) for i in range(count)]
    down = [(j, i) for i, j in up]
    first = lax.ppermute(part, ZH, up)
    third = lax.ppermute(part, ZH, down)
    second = lax.ppermute(first, ZH, up)
    return jnp.stack([first, third, second])


def other_core(value):
    return lax.ppermute(value, CORE, [(0, 1), (1, 0)])


def plane_gather(piece):
    count = lax.axis_size(PLANE)
    copies = jnp.broadcast_to(piece[None], (count,) + piece.shape)
    return lax.all_to_all(copies, PLANE, 0, 0, tiled=True)


def pack_kernel(q_ref, k_ref, v_ref, out_ref, gain_ref, mine_ref):
    depth, width = q_ref.shape
    out_depth, half = (out_ref.shape[0], out_ref.shape[1] // 2)
    for i, ref in enumerate((q_ref, k_ref, v_ref)):
        mine_ref[:, i * width : (i + 1) * width] = ref[...]
    begin = 3 * width
    mine_ref[:out_depth, begin : begin + half] = out_ref[:, :half]
    mine_ref[out_depth:, begin : begin + half] = out_ref[:, half:]
    mine_ref[:, begin + half :] = jnp.broadcast_to(gain_ref[...], (depth, gain_ref.shape[1]))


def assembly_kernel(
    place_ref, mine_ref, theirs_ref, far_ref, other_ref, joint_ref, out_ref, gain_ref
):
    step = pl.program_id(0)
    width = joint_ref.shape[1]
    half = out_ref.shape[1] // 2
    depth, rows = (out_ref.shape[0], gain_ref.shape[1])
    count = far_ref.shape[0]
    columns = far_ref.shape[3] - width // 2 - gain_ref.shape[2]
    across = out_ref.shape[1] // columns

    def near(ref):
        joint_ref[...] = ref[:, :width]
        out_ref[:, :half] = ref[:depth, width : width + half]
        out_ref[:, half:] = ref[depth:, width : width + half]
        gain_ref[0] = ref[:rows, width + half :]

    def distant(ref):
        for s in range(count):
            top, left = (s // 2 * rows, s % 2 * (width // 2))
            joint_ref[top : top + rows, left : left + width // 2] = ref[s, 0, :, : width // 2]
            top, left = (s // across * rows, s % across * columns)
            out_ref[top : top + rows, left : left + columns] = ref[
                s, 0, :, width // 2 : width // 2 + columns
            ]
        gain_ref[0] = ref[0, 0, :, width // 2 + columns :]

    pl.when(step == 0)(lambda: near(mine_ref))
    pl.when(step == 1)(lambda: near(theirs_ref))
    pl.when(jnp.logical_and(step > 1, step < 5))(lambda: distant(far_ref))
    pl.when(step >= 5)(lambda: distant(other_ref))


def assembled_weights(mine, theirs, far, other, width, out_shape):
    nz = lax.axis_size(ZH)
    zh, core = (lax.axis_index(ZH), lax.axis_index(CORE))
    peers = [zh, (zh + nz - 1) % nz, (zh + 1) % nz, (zh + 2) % nz]
    same = [2 * peer + core for peer in peers]
    swapped = [2 * peer + 1 - core for peer in peers]
    place = jnp.stack([same[0], swapped[0]] + same[1:] + swapped[1:])
    count, _, rows, total = far.shape
    depth = mine.shape[0]
    out_depth, model_width = out_shape
    gain_width = mine.shape[1] - width - model_width // 2
    whole = pl.BlockSpec(mine.shape, lambda i, place: (0, 0))

    def distant(first):
        return pl.BlockSpec(
            (count, 1, rows, total),
            lambda i, place: (0, jnp.clip(i - first, 0, 2), 0, 0),
        )

    shape = jax.ShapeDtypeStruct
    return pl.pallas_call(
        assembly_kernel,
        grid_spec=pltpu.PrefetchScalarGridSpec(
            num_scalar_prefetch=1,
            grid=(2 * nz,),
            in_specs=[whole, whole, distant(2), distant(5)],
            out_specs=[
                pl.BlockSpec((depth, width), lambda i, place: (place[i], 0)),
                pl.BlockSpec((out_depth, model_width), lambda i, place: (place[i], 0)),
                pl.BlockSpec((1, rows, gain_width), lambda i, place: (place[i], 0, 0)),
            ],
        ),
        out_shape=[
            shape((2 * nz * depth, width), BF16),
            shape((2 * nz * out_depth, model_width), BF16),
            shape((2 * nz, rows, gain_width), BF16),
        ],
        cost_estimate=pl.CostEstimate(flops=0, transcendentals=0, bytes_accessed=2**23),
    )(place, mine, theirs, far, other)


def gathered_weights(norm_gain, w_query, w_key, w_value, w_out):
    depth, hidden_width = w_query.shape
    half = w_out.shape[1] // 2
    part = column_gather(own_slices(norm_gain, w_query, w_key, w_value, w_out))
    far = plane_gather(part)
    mine = pl.pallas_call(
        pack_kernel,
        out_shape=jax.ShapeDtypeStruct((depth, 3 * hidden_width + half + depth), BF16),
    )(w_query, w_key, w_value, w_out, norm_gain[None])
    theirs = other_core(mine)
    other = other_core(far)
    joint, out_whole, gain = assembled_weights(
        mine, theirs, far, other, 3 * hidden_width, w_out.shape
    )
    return gain[:, 0, :].reshape(-1), joint, out_whole


def halved_gradient(attended, cotangent):
    nz = lax.axis_size(ZH)
    partial = jnp.einsum("sre,sru->eu", attended, cotangent, preferred_element_type=F32)
    width, model_width = partial.shape
    partial = partial.reshape(nz, 2, width // (2 * nz), model_width)
    first = lax.axis_index(CORE) == 0
    kept = jnp.where(first, partial[:, 0], partial[:, 1])
    sent = jnp.where(first, partial[:, 1], partial[:, 0])
    return (kept + other_core(sent)).astype(BF16)


def summed_gradient(half, total_samples):
    nx, ny, nz, nl = (lax.axis_size(X), lax.axis_size(Y), lax.axis_size(ZH), lax.axis_size(ZL))
    _, share, model_width = half.shape
    rows, columns = (share // nx, model_width // ny)
    half = jnp.stack([half[:, :, i * columns : (i + 1) * columns] for i in range(ny)])
    half = jnp.swapaxes(half.reshape(ny, nz, nx, rows, columns), 1, 2)
    half = half.reshape(ny * nx, nz, rows, columns)
    half = lax.all_to_all(half, (Y, X), 0, 0, tiled=True)
    part = jnp.sum(half.astype(F32), axis=0)
    part = jnp.broadcast_to(part[None], (nl, nz, rows, columns)).reshape(nl * nz, rows, columns)
    part = lax.all_to_all(part, COLUMN, 0, 0, tiled=True)
    part = jnp.sum(part, axis=0) / total_samples
    whole = plane_gather(part).reshape(nx, ny, rows, columns)
    return jnp.concatenate([whole[:, i].reshape(share, columns) for i in range(ny)], axis=1)


def shards(
    inputs, norm_gain, w_query, w_key, w_value, w_out, neighbors, slot_valid, output_cotangent
):
    samples, length, _ = inputs.shape
    block_count, _ = neighbors.shape
    block_len = length // block_count
    window_blocks = 3 * block_count
    groups = lax.axis_size(DOMAIN)
    up = [(i, i + 1) for i in range(groups - 1)]
    down = [(j, i) for i, j in up]
    below = lax.ppermute(inputs, DOMAIN, up)
    above = lax.ppermute(inputs, DOMAIN, down)
    gain, w_joint, w_full_out = gathered_weights(norm_gain, w_query, w_key, w_value, w_out)
    gain_float = gain.astype(F32)

    def inverse_of(rows):
        rows = rows.astype(F32)
        return lax.rsqrt(jnp.mean(rows * rows, axis=-1, keepdims=True) + EPSILON)

    inverse_rms = inverse_of(inputs)
    window = jnp.concatenate([below, inputs, above], axis=1)
    normed = (window.astype(F32) * inverse_of(window) * gain_float).astype(BF16)
    joint = jnp.einsum("sti,iy->sty", normed, w_joint, preferred_element_type=F32).astype(BF16)
    joint = pltpu.with_memory_space_constraint(joint, pltpu.HBM)
    d_attention = jnp.einsum(
        "stz,yz->sty", output_cotangent, w_full_out, preferred_element_type=F32
    ).astype(BF16)

    group = lax.axis_index(DOMAIN)
    local_index = neighbors - (group - 1) * block_count
    matches = jnp.logical_and(
        local_index[:, :, None] == jnp.arange(window_blocks, dtype=jnp.int32)[None, None, :],
        (slot_valid > 0)[:, :, None],
    )
    bias = jnp.where(jnp.any(matches, axis=1).T, 0.0, MASKED).astype(F32)
    bias = jnp.tile(jnp.repeat(bias, block_len, axis=1), (1, 2))[:, None, :]

    grads = (lax.ppermute(d_attention, DOMAIN, up), lax.ppermute(d_attention, DOMAIN, down))
    attended, stats = forward_attention(bias, joint)
    half = halved_gradient(attended, output_cotangent)
    members = lax.axis_size(MEMBER)
    grad_wout = summed_gradient(half, samples * members)
    d_query, own, stats = query_gradient(bias, joint, d_attention, stats)
    side_stats = (lax.ppermute(stats, DOMAIN, up), lax.ppermute(stats, DOMAIN, down))
    d_key, d_value = key_gradient(joint, grads, side_stats, own)
    attn_out = jnp.einsum(
        "sty,yb->stb", attended, w_full_out, preferred_element_type=F32
    ).astype(BF16)
    d_joint = jnp.concatenate([d_query, d_key, d_value], axis=-1)
    d_normed = jnp.einsum("sty,iy->sti", d_joint, w_joint, preferred_element_type=F32)
    inputs_float = inputs.astype(F32)
    scaled = d_normed * gain_float
    inner = jnp.mean(scaled * inputs_float, axis=-1, keepdims=True)
    d_input = inverse_rms * scaled - inputs_float * inverse_rms**3 * inner
    return attn_out, d_input.astype(BF16), grad_wout


def solution(mesh):
    fine = Mesh(mesh.devices.reshape(4, 4, 4, 4, 2), (X, Y, ZL, ZH, CORE))
    placed = (
        P(MEMBER, DOMAIN, None),
        P(MEMBER),
        P(MEMBER, None),
        P(MEMBER, None),
        P(MEMBER, None),
        P(MEMBER, None),
        P(DOMAIN, None),
        P(DOMAIN, None),
        P(MEMBER, DOMAIN, None),
    )

    return jax.shard_map(
        shards,
        mesh=fine,
        in_specs=placed,
        out_specs=(P(MEMBER, DOMAIN, None), P(MEMBER, DOMAIN, None), P(MEMBER, None)),
        check_vma=False,
    )
```

```python
import jax
import jax.numpy as jnp
from jax import lax
from jax.experimental import pallas as pl
from jax.experimental.pallas import tpu as pltpu
from jax.sharding import Mesh
from jax.sharding import PartitionSpec as P


HEAD_DIM = 64
PAIR = 2 * HEAD_DIM
SCALE = HEAD_DIM**-0.5
EPSILON = 1e-06
MASKED = -1e30
X, Y, ZL, ZH, CORE = "x", "y", "zl", "zh", "core"
DOMAIN = (X, Y, ZL)
MEMBER = (ZH, CORE)
PLANE = (X, Y)
COLUMN = (ZL, ZH)
BF16, F32 = jnp.bfloat16, jnp.float32


def contract(a, b, da, db):
    return lax.dot_general(a, b, (((da,), (db,)), ((), ())), preferred_element_type=F32)


def head_lanes():
    return lax.broadcasted_iota(jnp.int32, (1, PAIR), 1) < HEAD_DIM


def stacked(both, scale=1.0):
    near = head_lanes()
    both = both * jnp.asarray(scale, both.dtype)
    zero = jnp.zeros_like(both)
    return jnp.concatenate([jnp.where(near, both, zero), jnp.where(near, zero, both)], axis=0)


def merged(columns):
    both = columns.T
    rows = both.shape[0] // 2
    return jnp.where(head_lanes(), both[:rows], both[rows:])


def masked_scores(bias, key, query):
    blocks = bias.shape[0]
    span, columns = (key.shape[0], query.shape[0])
    scores = contract(key, query, 1, 1).reshape(blocks, span // blocks, columns)
    return (scores + bias).reshape(span, columns)


def forward_kernel(bias_ref, q_ref, k_ref, v_ref, att_ref, stat_ref):
    scores = masked_scores(bias_ref[...], k_ref[0], stacked(q_ref[0], SCALE))
    row_max = jnp.max(scores, axis=0, keepdims=True)
    shifted = jnp.exp(scores - row_max)
    total = jnp.sum(shifted, axis=0, keepdims=True)
    prob_bf = (shifted * (1.0 / total)).astype(BF16)
    att_ref[0] = merged(contract(v_ref[0], prob_bf, 0, 0)).astype(BF16)
    stat_ref[0, 0] = row_max + jnp.log(total)


def probability(bias, key, query, stats):
    return jnp.exp(masked_scores(bias, key, query) - stats[0:1])


def query_kernel(bias_ref, q_ref, k_ref, v_ref, g_ref, stat_ref, dq_ref, own_ref, sent_ref):
    rows = q_ref.shape[1]
    query, key, value, grad = (stacked(q_ref[0], SCALE), k_ref[0], v_ref[0], stacked(g_ref[0]))
    stats = stat_ref[0, 0]
    prob = probability(bias_ref[...], key, query, stats)
    d_prob = contract(value, grad, 1, 1)
    delta = jnp.sum(prob * d_prob, axis=0, keepdims=True)
    d_score = (prob * (d_prob - delta)).astype(BF16)
    dq_ref[0] = (merged(contract(key, d_score, 0, 0)) * SCALE).astype(BF16)
    own_ref[0, 0] = contract(d_score[rows : 2 * rows], query, 1, 0)
    own_ref[1, 0] = contract(prob[rows : 2 * rows].astype(BF16), grad, 1, 0)
    third = bias_ref.shape[0] // 3
    sent_ref[0, 0, 0:1, :] = stats
    sent_ref[0, 0, 1:2, :] = delta
    for i in range(third):
        sent_ref[0, 0, 2 + i : 3 + i, :] = bias_ref[2 * third + i]
        sent_ref[0, 0, 2 + third + i : 3 + third + i, :] = bias_ref[i]


def key_kernel(
    low_q_ref,
    high_q_ref,
    k_ref,
    v_ref,
    low_g_ref,
    high_g_ref,
    low_stat_ref,
    high_stat_ref,
    own_ref,
    dk_ref,
    dv_ref,
):
    key, value = (k_ref[0], v_ref[0])
    d_key, d_value = (own_ref[0, 0], own_ref[1, 0])
    sides = ((low_q_ref, low_g_ref, low_stat_ref), (high_q_ref, high_g_ref, high_stat_ref))
    for side, (q_ref, g_ref, stat_ref) in enumerate(sides):
        query, grad, stats = (stacked(q_ref[0], SCALE), stacked(g_ref[0]), stat_ref[0, 0])
        third = (stats.shape[0] - 2) // 2
        first = 2 + side * third
        bias = jnp.stack([stats[first + i : first + i + 1] for i in range(third)])
        prob = probability(bias, key, query, stats)
        d_score = (prob * (contract(value, grad, 1, 1) - stats[1:2])).astype(BF16)
        d_key += contract(d_score, query, 1, 0).astype(BF16).astype(F32)
        d_value += contract(prob.astype(BF16), grad, 1, 0).astype(BF16).astype(F32)
    dk_ref[0] = d_key.astype(BF16)
    dv_ref[0] = d_value.astype(BF16)


class Plan:
    def __init__(self, joint):
        samples, span, width = joint.shape
        self.rows, self.width, self.span = (span // 3, width // 3, span)
        self.samples, self.pairs = (samples, width // 3 // PAIR)
        self.grid = (samples, self.pairs)
        self.narrow = pl.BlockSpec((1, self.rows, PAIR), lambda s, h: (s, 0, h))
        self.split = pl.BlockSpec((2, 1, self.rows, PAIR), lambda s, h: (0, s, 0, h))

    def joint(self, kind, third=None):
        first = kind * self.pairs
        if third is None:
            return pl.BlockSpec((1, self.span, PAIR), lambda s, h: (s, 0, h + first))
        return pl.BlockSpec((1, self.rows, PAIR), lambda s, h: (s, third, h + first))

    def bias(self, bias):
        return pl.BlockSpec(bias.shape, lambda s, h: (0, 0, 0))

    def stat(self, count):
        return pl.BlockSpec((1, 1, count, 2 * self.rows), lambda s, h: (s, h, 0, 0))

    def stat_shape(self, count):
        return jax.ShapeDtypeStruct((self.samples, self.pairs, count, 2 * self.rows), F32)

    def narrow_shape(self):
        return jax.ShapeDtypeStruct((self.samples, self.rows, self.width), BF16)

    def call(self, kernel, products, in_specs, out_specs, out_shape):
        work = self.samples * self.rows * self.span * self.width
        return pl.pallas_call(
            kernel,
            grid=self.grid,
            in_specs=in_specs,
            out_specs=out_specs,
            out_shape=out_shape,
            cost_estimate=pl.CostEstimate(
                flops=2 * products * work,
                transcendentals=work // HEAD_DIM,
                bytes_accessed=3 * products * self.samples * self.rows * self.width,
            ),
            compiler_params=pltpu.CompilerParams(vmem_limit_bytes=16 * 2**20),
        )


def forward_attention(bias, joint):
    plan = Plan(joint)
    given = [plan.bias(bias), plan.joint(0, 1), plan.joint(1), plan.joint(2)]
    outs = ([plan.narrow, plan.stat(1)], [plan.narrow_shape(), plan.stat_shape(1)])
    return plan.call(forward_kernel, 2, given, *outs)(bias, joint, joint, joint)


def query_gradient(bias, joint, grad, stats):
    plan = Plan(joint)
    count = 2 + 2 * (bias.shape[0] // 3)
    given = [plan.bias(bias), plan.joint(0, 1), plan.joint(1), plan.joint(2)]
    given += [plan.narrow, plan.stat(1)]
    own = jax.ShapeDtypeStruct((2, plan.samples, plan.rows, plan.width), F32)
    outs = (
        [plan.narrow, plan.split, plan.stat(count)],
        [plan.narrow_shape(), own, plan.stat_shape(count)],
    )
    return plan.call(query_kernel, 4, given, *outs)(bias, joint, joint, joint, grad, stats)


def key_gradient(joint, grads, stats, own):
    plan = Plan(joint)
    given = [plan.joint(0, 0), plan.joint(0, 2), plan.joint(1, 1), plan.joint(2, 1)]
    given += [plan.narrow] * 2 + [plan.stat(stats[0].shape[2])] * 2 + [plan.split]
    outs = ([plan.narrow] * 2, [plan.narrow_shape()] * 2)
    call = plan.call(key_kernel, 3, given, *outs)
    return call(joint, joint, joint, joint, *grads, *stats, own)


def slice_kernel(place_ref, q_ref, k_ref, v_ref, out_ref, gain_ref, part_ref):
    rows, width = q_ref.shape
    half = width // 2
    columns = out_ref.shape[1]

    @pl.when(place_ref[1] == 0)
    def _():
        part_ref[:, :width] = q_ref[...]
        part_ref[:, width : width + half] = k_ref[:, :half]

    @pl.when(place_ref[1] != 0)
    def _():
        part_ref[:, :half] = k_ref[:, half:]
        part_ref[:, half : half + width] = v_ref[...]

    begin = width + half
    part_ref[:, begin : begin + columns] = out_ref[...]
    part_ref[:, begin + columns :] = jnp.broadcast_to(gain_ref[...], (rows, gain_ref.shape[1]))


def own_slices(norm_gain, w_query, w_key, w_value, w_out):
    nx, ny = (lax.axis_size(X), lax.axis_size(Y))
    xi, yi = (lax.axis_index(X), lax.axis_index(Y))
    depth, width = w_query.shape
    rows, columns = (w_out.shape[0] // nx, w_out.shape[1] // ny)
    number = xi * ny + yi
    place = jnp.stack([number // 2, number % 2, xi, yi])
    band = pl.BlockSpec((rows, width), lambda i, place: (place[0], 0))
    total = width + width // 2 + columns + depth
    return pl.pallas_call(
        slice_kernel,
        grid_spec=pltpu.PrefetchScalarGridSpec(
            num_scalar_prefetch=1,
            grid=(1,),
            in_specs=[
                band,
                band,
                band,
                pl.BlockSpec((rows, columns), lambda i, place: (place[2], place[3])),
                pl.BlockSpec((1, depth), lambda i, place: (0, 0)),
            ],
            out_specs=pl.BlockSpec((rows, total), lambda i, place: (0, 0)),
        ),
        out_shape=jax.ShapeDtypeStruct((rows, total), BF16),
    )(place, w_query, w_key, w_value, w_out, norm_gain[None])


def column_gather(part):
    count = lax.axis_size(ZH)
    up = [(i, (i + 1) % count) for i in range(count)]
    down = [(j, i) for i, j in up]
    first = lax.ppermute(part, ZH, up)
    third = lax.ppermute(part, ZH, down)
    second = lax.ppermute(first, ZH, up)
    return jnp.stack([first, third, second])


def other_core(value):
    return lax.ppermute(value, CORE, [(0, 1), (1, 0)])


def plane_gather(piece):
    count = lax.axis_size(PLANE)
    copies = jnp.broadcast_to(piece[None], (count,) + piece.shape)
    return lax.all_to_all(copies, PLANE, 0, 0, tiled=True)


def pack_kernel(q_ref, k_ref, v_ref, out_ref, gain_ref, mine_ref):
    depth, width = q_ref.shape
    out_depth, half = (out_ref.shape[0], out_ref.shape[1] // 2)
    for i, ref in enumerate((q_ref, k_ref, v_ref)):
        mine_ref[:, i * width : (i + 1) * width] = ref[...]
    begin = 3 * width
    mine_ref[:out_depth, begin : begin + half] = out_ref[:, :half]
    mine_ref[out_depth:, begin : begin + half] = out_ref[:, half:]
    mine_ref[:, begin + half :] = jnp.broadcast_to(gain_ref[...], (depth, gain_ref.shape[1]))


def chosen(step, refs, near, distant):
    mine_ref, theirs_ref, far_ref, other_ref = refs
    pl.when(step == 0)(lambda: near(mine_ref))
    pl.when(step == 1)(lambda: near(theirs_ref))
    pl.when(jnp.logical_and(step > 1, step < 5))(lambda: distant(far_ref))
    pl.when(step >= 5)(lambda: distant(other_ref))


def joint_kernel(place_ref, *refs):
    blocks, gains, (joint_ref, gain_ref) = (refs[:4], refs[4:8], refs[8:])
    rows = gain_ref.shape[1]
    half = joint_ref.shape[1] // 2

    def near(ref):
        joint_ref[...] = ref[...]

    def distant(ref):
        for s in range(ref.shape[0]):
            top, left = (s // 2 * rows, s % 2 * half)
            joint_ref[top : top + rows, left : left + half] = ref[s, 0]

    def near_gain(ref):
        gain_ref[0] = ref[...]

    def distant_gain(ref):
        gain_ref[0] = ref[0, 0]

    chosen(pl.program_id(0), blocks, near, distant)
    chosen(pl.program_id(0), gains, near_gain, distant_gain)


def output_kernel(place_ref, *refs):
    blocks, out_ref = (refs[:4], refs[4])
    depth, width = out_ref.shape
    rows, columns = blocks[2].shape[2:]
    across = width // columns

    def near(ref):
        out_ref[:, : width // 2] = ref[:depth, :]
        out_ref[:, width // 2 :] = ref[depth:, :]

    def distant(ref):
        for s in range(ref.shape[0]):
            top, left = (s // across * rows, s % across * columns)
            out_ref[top : top + rows, left : left + columns] = ref[s, 0]

    chosen(pl.program_id(0), blocks, near, distant)


def assembled(kernel, sources, blocks, out_specs, out_shape):
    nz = lax.axis_size(ZH)
    zh, core = (lax.axis_index(ZH), lax.axis_index(CORE))
    peers = [zh, (zh + nz - 1) % nz, (zh + 1) % nz, (zh + 2) % nz]
    same = [2 * peer + core for peer in peers]
    swapped = [2 * peer + 1 - core for peer in peers]
    place = jnp.stack([same[0], swapped[0]] + same[1:] + swapped[1:])
    specs, operands = ([], [])
    for near, near_at, distant, distant_at in blocks:
        for first in (None, None, 2, 5):
            if first is None:
                specs.append(pl.BlockSpec(near, lambda i, place, at=near_at: (0, at)))
            else:
                specs.append(
                    pl.BlockSpec(
                        distant,
                        lambda i, place, at=distant_at, first=first: (
                            0,
                            jnp.clip(i - first, 0, 2),
                            0,
                            at,
                        ),
                    )
                )
        operands += sources
    return pl.pallas_call(
        kernel,
        grid_spec=pltpu.PrefetchScalarGridSpec(
            num_scalar_prefetch=1, grid=(2 * nz,), in_specs=specs, out_specs=out_specs
        ),
        out_shape=out_shape,
        cost_estimate=pl.CostEstimate(flops=0, transcendentals=0, bytes_accessed=2**23),
        compiler_params=pltpu.CompilerParams(vmem_limit_bytes=16 * 2**20),
    )(place, *operands)


def gathered_weights(norm_gain, w_query, w_key, w_value, w_out):
    depth, hidden_width = w_query.shape
    half = w_out.shape[1] // 2
    part = column_gather(own_slices(norm_gain, w_query, w_key, w_value, w_out))
    far = plane_gather(part)
    mine = pl.pallas_call(
        pack_kernel,
        out_shape=jax.ShapeDtypeStruct((depth, 3 * hidden_width + half + depth), BF16),
        compiler_params=pltpu.CompilerParams(vmem_limit_bytes=8 * 2**20),
    )(w_query, w_key, w_value, w_out, norm_gain[None])
    theirs = other_core(mine)
    other = other_core(far)
    sources = [mine, theirs, far, other]
    count, _, rows, total = far.shape
    members, width = (lax.axis_size(MEMBER), 3 * hidden_width)
    columns = total - width // 2 - depth
    shape = jax.ShapeDtypeStruct
    joint, gain = assembled(
        joint_kernel,
        sources,
        [
            ((depth, width), 0, (count, 1, rows, width // 2), 0),
            ((rows, depth), (width + half) // depth, (1, 1, rows, depth), total // depth - 1),
        ],
        [
            pl.BlockSpec((depth, width), lambda i, place: (place[i], 0)),
            pl.BlockSpec((1, rows, depth), lambda i, place: (place[i], 0, 0)),
        ],
        [shape((members * depth, width), BF16), shape((members, rows, depth), BF16)],
    )
    out_whole = assembled(
        output_kernel,
        sources,
        [((depth, half), width // half, (count, 1, rows, columns), width // 2 // columns)],
        pl.BlockSpec(w_out.shape, lambda i, place: (place[i], 0)),
        shape((members * w_out.shape[0], w_out.shape[1]), BF16),
    )
    return gain[:, 0, :].reshape(-1), joint, out_whole


def halved_gradient(attended, cotangent):
    nz = lax.axis_size(ZH)
    partial = jnp.einsum("sre,sru->eu", attended, cotangent, preferred_element_type=F32)
    width, model_width = partial.shape
    partial = partial.reshape(nz, 2, width // (2 * nz), model_width)
    first = lax.axis_index(CORE) == 0
    kept = jnp.where(first, partial[:, 0], partial[:, 1])
    sent = jnp.where(first, partial[:, 1], partial[:, 0])
    received = other_core(sent)
    return (kept + received).astype(BF16)


def summed_gradient(half, total_samples):
    nx, ny, nz, nl = (lax.axis_size(X), lax.axis_size(Y), lax.axis_size(ZH), lax.axis_size(ZL))
    _, share, model_width = half.shape
    rows, columns = (share // nx, model_width // ny)
    half = jnp.stack([half[:, :, i * columns : (i + 1) * columns] for i in range(ny)])
    half = jnp.swapaxes(half.reshape(ny, nz, nx, rows, columns), 1, 2)
    half = half.reshape(ny * nx, nz, rows, columns)
    half = lax.all_to_all(half, (Y, X), 0, 0, tiled=True)
    part = jnp.sum(half.astype(F32), axis=0)
    part = jnp.broadcast_to(part[None], (nl, nz, rows, columns)).reshape(nl * nz, rows, columns)
    part = lax.all_to_all(part, COLUMN, 0, 0, tiled=True)
    part = jnp.sum(part, axis=0) / total_samples
    whole = plane_gather(part).reshape(nx, ny, rows, columns)
    return jnp.concatenate([whole[:, i].reshape(share, columns) for i in range(ny)], axis=1)


def shards(
    inputs, norm_gain, w_query, w_key, w_value, w_out, neighbors, slot_valid, output_cotangent
):
    samples, length, _ = inputs.shape
    block_count, _ = neighbors.shape
    block_len = length // block_count
    window_blocks = 3 * block_count
    groups = lax.axis_size(DOMAIN)
    up = [(i, i + 1) for i in range(groups - 1)]
    down = [(j, i) for i, j in up]
    below = lax.ppermute(inputs, DOMAIN, up)
    above = lax.ppermute(inputs, DOMAIN, down)
    gain, w_joint, w_full_out = gathered_weights(norm_gain, w_query, w_key, w_value, w_out)
    gain_float = gain.astype(F32)

    def inverse_of(rows):
        rows = rows.astype(F32)
        return lax.rsqrt(jnp.mean(rows * rows, axis=-1, keepdims=True) + EPSILON)

    inverse_rms = inverse_of(inputs)
    window = jnp.concatenate([below, inputs, above], axis=1)
    normed = (window.astype(F32) * inverse_of(window) * gain_float).astype(BF16)
    joint = jnp.einsum("sti,iy->sty", normed, w_joint, preferred_element_type=F32).astype(BF16)
    joint = pltpu.with_memory_space_constraint(joint, pltpu.HBM)
    d_attention = jnp.einsum(
        "stz,yz->sty", output_cotangent, w_full_out, preferred_element_type=F32
    ).astype(BF16)

    group = lax.axis_index(DOMAIN)
    local_index = neighbors - (group - 1) * block_count
    matches = jnp.logical_and(
        local_index[:, :, None] == jnp.arange(window_blocks, dtype=jnp.int32)[None, None, :],
        (slot_valid > 0)[:, :, None],
    )
    bias = jnp.where(jnp.any(matches, axis=1).T, 0.0, MASKED).astype(F32)
    bias = jnp.tile(jnp.repeat(bias, block_len, axis=1), (1, 2))[:, None, :]

    grads = (lax.ppermute(d_attention, DOMAIN, up), lax.ppermute(d_attention, DOMAIN, down))
    attended, stats = forward_attention(bias, joint)
    half = halved_gradient(attended, output_cotangent)
    members = lax.axis_size(MEMBER)
    grad_wout = summed_gradient(half, samples * members)
    d_query, own, stats = query_gradient(bias, joint, d_attention, stats)
    side_stats = (lax.ppermute(stats, DOMAIN, up), lax.ppermute(stats, DOMAIN, down))
    d_key, d_value = key_gradient(joint, grads, side_stats, own)
    attn_out = jnp.einsum(
        "sty,yb->stb", attended, w_full_out, preferred_element_type=F32
    ).astype(BF16)
    d_joint = jnp.concatenate([d_query, d_key, d_value], axis=-1)
    d_normed = jnp.einsum("sty,iy->sti", d_joint, w_joint, preferred_element_type=F32)
    inputs_float = inputs.astype(F32)
    scaled = d_normed * gain_float
    inner = jnp.mean(scaled * inputs_float, axis=-1, keepdims=True)
    d_input = inverse_rms * scaled - inputs_float * inverse_rms**3 * inner
    return attn_out, d_input.astype(BF16), grad_wout


def solution(mesh):
    fine = Mesh(mesh.devices.reshape(4, 4, 4, 4, 2), (X, Y, ZL, ZH, CORE))
    placed = (
        P(MEMBER, DOMAIN, None),
        P(MEMBER),
        P(MEMBER, None),
        P(MEMBER, None),
        P(MEMBER, None),
        P(MEMBER, None),
        P(DOMAIN, None),
        P(DOMAIN, None),
        P(MEMBER, DOMAIN, None),
    )

    return jax.shard_map(
        shards,
        mesh=fine,
        in_specs=placed,
        out_specs=(P(MEMBER, DOMAIN, None), P(MEMBER, DOMAIN, None), P(MEMBER, None)),
        check_vma=False,
    )
```
